32 devices in a mesh: seq: 8 (over z, x), head: 4 (over y, core).
Axes of the slice: x: 2, y: 2, z: 4, core: 2. Of those that a mesh axis runs over, the one named last changes fastest.
Arguments:
- tokens: bfloat16 [1024, 2048], P('seq', 'head'), may hold values from -6 to 6
- norm_gain: float32 [2048], replicated, may hold values from 0.1 to 1.9
- query_weight: bfloat16 [2048, 2048], P(None, 'head')
- key_weight: bfloat16 [2048, 256], replicated, may hold values from -0.125 to 0.125
- value_weight: bfloat16 [2048, 256], replicated, may hold values from -0.125 to 0.125
- window_lengths: int32 [8], replicated, may hold values from 1 to 256, 1024 in all
- is_caption: int32 [1024], P('seq'), may hold values 0 or 1
- span_blocks: int32 [8, 2], P('seq'), may hold values from 0 to 7, as said below
Outputs:
- attended: bfloat16 [1024, 2048], P('seq', 'head')
The draws below stay inside these ranges and needn't reach their ends.
Inputs may be any that keep to these rules, and one draw needn't show every extreme that they name: `window_lengths`: window lengths are whole numbers summing to 1024, the largest exactly 256. `is_caption`: 1 marks a caption token, 0 a visual token. `span_blocks`: row b holds first and last key block of one event span: first <= last <= first + 1 and first <= 6; some span has exactly 2 blocks.
All inputs are finite; a program needn't handle non-finite values. No bound on the sum of `is_caption` on one device may be relied on, other than what follows from the above.
Results may differ from the reference program's by a relative error of at most 0.019.
The reference program's roundings to bfloat16 on the way count: a program that leaves them out, or rounds other values in their place, can miss the bound.
Values may be sent and summed in bfloat16 or wider, within the bound.
No kernel may reach another device: no remote copies, remote signals or barrier semaphores. Data moves between devices by JAX's collectives and lax.ppermute only.
A program may use at most 64 MiB of HBM per device.

```python
import math
import jax
import jax.numpy as jnp
import numpy as np
from jax import lax

D = 2048
H = 16
KV = 2
HD = 128
BLOCK = 128
TOKENS = 1024
NBLK = 8
WINDOW = 256
WBACK = 2
SPAN_MOST = 2
NWIN = 8


def draw_query_weight(key, part):
    matrix = jax.random.normal(key, (D, H * HD), jnp.float32) * (6.0 / D) ** 0.5
    return matrix.astype(jnp.bfloat16)


def draw_span_blocks(key, part):
    total_blocks = TOKENS // BLOCK
    first_key = jax.random.fold_in(key, 11)
    second_key = jax.random.fold_in(key, 12)
    third_key = jax.random.fold_in(key, 13)
    starts = jax.random.randint(first_key, (total_blocks,), 0, total_blocks - SPAN_MOST + 1)
    widths = jax.random.randint(second_key, (total_blocks,), 1, SPAN_MOST + 1)
    chosen = jax.random.randint(third_key, (), 0, total_blocks)
    widths = jnp.where(jnp.arange(total_blocks) == chosen, SPAN_MOST, widths)
    return jnp.stack([starts, starts + widths - 1], 1).astype(jnp.int32)


def set_ends(values, stream_key, smallest, high):
    longest = values.shape.index(max(values.shape))
    spots = []
    for shift in (0, 1):
        where = [jax.random.randint(jax.random.fold_in(stream_key, axis), (), 0, length) for axis, length in enumerate(values.shape)]
        where[longest] = (where[longest] + shift) % values.shape[longest]
        spots.append(tuple(where))
    return values.at[spots[0]].set(smallest).at[spots[1]].set(high)


def steps_of(key, shape, split, smallest, largest):
    loudness = 1.0
    for axis_at, blocks in split:
        draws = jax.random.uniform(jax.random.fold_in(jax.random.fold_in(key, 6), axis_at), (blocks,), jnp.float32, smallest / len(split), largest / len(split))
        loudness = loudness * jnp.repeat(jnp.exp(draws), shape[axis_at] // blocks).reshape((-1,) + (1,) * (len(shape) - 1 - axis_at))
    return loudness


def profile(count, total, most, slope):
    weights = [(1 << 20) // math.isqrt(standing ** slope) + 1 for standing in range(2, count + 1)]
    rest, counts = total - most - (count - 1), [1] * (count - 1)
    while rest > 0:
        movable = [i for i in range(count - 1) if counts[i] < most]
        mass, left = sum([weights[i] for i in movable]), rest
        for i in movable:
            more = min(most - counts[i], max(1, left * weights[i] // mass), rest)
            counts[i] = counts[i] + more
            rest = rest - more
    return np.array([most] + counts)


def ragged(rng, amount, total, bound, lean):
    if amount == 2:
        one = jax.random.randint(rng, (), max(1, total - bound), min(bound, total - 1) + 1)
        return jnp.stack([one, total - one])
    sizes = jnp.asarray(profile(amount, total, bound, lean), jnp.int32)
    couples = (amount - 1) // 2
    giver, receiver = sizes[1:1 + 2 * couples:2], sizes[2:2 + 2 * couples:2]
    slack = jnp.minimum(giver - 1, bound - receiver)
    passed = jax.random.randint(jax.random.fold_in(rng, 1), (couples,), 0, 1 << 20) % (slack + 1)
    sizes = sizes.at[1:1 + 2 * couples:2].set(giver - passed).at[2:2 + 2 * couples:2].set(receiver + passed)
    return sizes[jax.random.permutation(jax.random.fold_in(rng, 2), amount)]


def noise(rng, extent, width, limit, pieces=(), kind=jnp.bfloat16):
    values = jax.random.normal(rng, extent, jnp.float32) * width
    if len(pieces) > 0:
        values = steps_of(rng, extent, pieces, -0.22, 0.18) * values
    return jnp.clip(values, min=-limit, max=limit).astype(kind)


def setup_inputs(seed: int = 0) -> dict:
    splits = jax.random.split(jax.random.key(seed), 9)
    return {
        "tokens": noise(splits[0], (TOKENS, D), 1.0, 6.0, ((0, 8), (1, 4))),
        "norm_gain": jnp.clip(1.0 + 0.18 * jax.random.normal(splits[1], (D,), jnp.float32), 0.1, 1.9),
        "query_weight": draw_query_weight(jax.random.fold_in(splits[8], 71), 0),
        "key_weight": noise(splits[3], (D, KV * HD), D ** -0.5, 0.125),
        "value_weight": noise(splits[4], (D, KV * HD), D ** -0.5, 0.125),
        "window_lengths": ragged(splits[5], NWIN, TOKENS, WINDOW, 1).astype(jnp.int32),
        "is_caption": set_ends((jax.random.randint(splits[6], (TOKENS,), 0, 3) < 1).astype(jnp.int32), jax.random.fold_in(splits[6], 1), 0, 1),
        "span_blocks": draw_span_blocks(jax.random.fold_in(splits[8], 71), 0),
    }


norm_eps = 1e-05
rope_base = 500000.0

def rotate(vectors, position):
    half_size = vectors.shape[-1] // 2
    frequency = rope_base ** (-jnp.arange(half_size, dtype=jnp.float32) * 2.0 / vectors.shape[-1])
    angles = position.astype(jnp.float32)[:, None] * frequency[None, :]
    cosine = jnp.cos(angles)[:, None, :]
    sine_part = jnp.sin(angles)[:, None, :]
    first_half = vectors[..., :half_size]
    second_half = vectors[..., half_size:]
    return jnp.concatenate([first_half * cosine - second_half * sine_part, second_half * cosine + first_half * sine_part], -1)

def rms_normed(tokens, norm_gain):
    hidden = tokens.astype(jnp.float32)
    scale = lax.rsqrt(lax.optimization_barrier(jnp.mean(hidden * hidden, -1, keepdims=True)) + norm_eps)
    return (hidden * scale * norm_gain.astype(jnp.float32)[None, :]).astype(jnp.bfloat16)

def window_starts(window_lengths, position):
    window_ends = jnp.cumsum(window_lengths).astype(jnp.int32)
    begins = window_ends - window_lengths
    within = (begins[None, :] <= position[:, None]) & (position[:, None] < window_ends[None, :])
    return lax.optimization_barrier(jnp.sum(jnp.where(within, begins[None, :], 0), 1)).astype(jnp.int32)

def inside(first_row, row_pos, key_pos):
    return (first_row[:, None] <= key_pos[None, :]) & (key_pos[None, :] <= row_pos[:, None])

def reference(tokens, norm_gain, query_weight, key_weight, value_weight, window_lengths, is_caption, span_blocks):
    token_count = tokens.shape[0]
    group_size = H // KV
    normed = rms_normed(tokens, norm_gain)
    position = jnp.arange(token_count, dtype=jnp.int32)
    queries = jnp.dot(normed, query_weight, preferred_element_type=jnp.float32).reshape(token_count, H, HD)
    queries = (rotate(queries, position) * HD ** (-0.5)).astype(jnp.bfloat16)
    key_rows = jnp.dot(normed, key_weight, preferred_element_type=jnp.float32).reshape(token_count, KV, HD)
    key_rows = rotate(key_rows, position).astype(jnp.bfloat16)
    value_rows = jnp.dot(normed, value_weight, preferred_element_type=jnp.float32).astype(jnp.bfloat16).reshape(token_count, KV, HD)
    window_first = window_starts(window_lengths, position)
    padding = jnp.zeros((WBACK * BLOCK, KV, HD), jnp.bfloat16)
    padded_keys = jnp.concatenate([padding, key_rows], 0)
    padded_values = jnp.concatenate([padding, value_rows], 0)

    def one_block(block_index):
        block_base = (block_index * BLOCK).astype(jnp.int32)
        row_pos = block_base + jnp.arange(BLOCK, dtype=jnp.int32)
        block_queries = lax.dynamic_slice_in_dim(queries, block_base, BLOCK, 0).reshape(BLOCK, KV, group_size, HD)
        near_count = (WBACK + 1) * BLOCK
        near_keys = lax.dynamic_slice_in_dim(padded_keys, block_base, near_count, 0)
        near_values = lax.dynamic_slice_in_dim(padded_values, block_base, near_count, 0)
        near_pos = block_base - WBACK * BLOCK + jnp.arange(near_count, dtype=jnp.int32)
        span_first = span_blocks[block_index, 0].astype(jnp.int32)
        finish = span_blocks[block_index, 1].astype(jnp.int32)
        far_keys = lax.dynamic_slice_in_dim(key_rows, span_first * BLOCK, SPAN_MOST * BLOCK, 0)
        far_values = lax.dynamic_slice_in_dim(value_rows, span_first * BLOCK, SPAN_MOST * BLOCK, 0)
        far_pos = span_first * BLOCK + jnp.arange(SPAN_MOST * BLOCK, dtype=jnp.int32)
        first_row = lax.dynamic_slice_in_dim(window_first, block_base, BLOCK, 0)
        caption_row = lax.dynamic_slice_in_dim(is_caption, block_base, BLOCK, 0) == 1
        near_ok = inside(first_row, row_pos, near_pos)
        far_ok = (far_pos[None, :] // BLOCK <= finish) & caption_row[:, None] & ~inside(first_row, row_pos, far_pos)
        all_keys = jnp.concatenate([near_keys, far_keys], 0)
        all_values = jnp.concatenate([near_values, far_values], 0)
        allowed = jnp.concatenate([near_ok, far_ok], 1)
        scores = jnp.einsum('rkgd,nkd->rkgn', block_queries.astype(jnp.float32), all_keys.astype(jnp.float32))
        scores = jnp.where(allowed[:, None, None, :], scores, -jnp.inf)
        highest = lax.optimization_barrier(jnp.max(scores, -1, keepdims=True))
        weights = jnp.exp(scores - highest)
        denominator = lax.optimization_barrier(jnp.sum(weights, -1))
        rounded = lax.optimization_barrier(weights.astype(jnp.bfloat16))
        mixed = jnp.einsum('rkgn,nkd->rkgd', rounded.astype(jnp.float32), all_values.astype(jnp.float32))
        return (mixed / denominator[..., None]).reshape(BLOCK, H * HD).astype(jnp.bfloat16)
    outputs = lax.map(one_block, jnp.arange(NBLK, dtype=jnp.int32))
    return outputs.reshape(token_count, H * HD)
```

```python
import functools

import jax
import jax.numpy as jnp
from jax import lax
from jax.experimental import pallas as pl
from jax.experimental.pallas import tpu as pltpu
from jax.sharding import PartitionSpec as P

H = 16
KV = 2
HD = 128
BLOCK = 128


norm_eps = 1e-05
rope_base = 500000.0
window_cap = 4096
span_cap = 8
slice_blocks = 8
lowest_start = -1e30


def rotate(vectors, position):
    half_size = vectors.shape[-1] // 2
    frequency = rope_base ** (-jnp.arange(half_size, dtype=jnp.float32) * 2.0 / vectors.shape[-1])
    angles = position.astype(jnp.float32)[:, None] * frequency[None, :]
    cosine = jnp.cos(angles)[:, None, :]
    sine_part = jnp.sin(angles)[:, None, :]
    first_half = vectors[..., :half_size]
    second_half = vectors[..., half_size:]
    return jnp.concatenate(
        [
            first_half * cosine - second_half * sine_part,
            second_half * cosine + first_half * sine_part,
        ],
        -1,
    )


def rms_normed(tokens, norm_gain):
    hidden = tokens.astype(jnp.float32)
    scale = lax.rsqrt(jnp.mean(hidden * hidden, -1, keepdims=True) + norm_eps)
    return (hidden * scale * norm_gain[None, :]).astype(jnp.bfloat16)


def window_starts(window_lengths, position):
    window_ends = jnp.cumsum(window_lengths)
    begins = window_ends - window_lengths
    within = (begins[None, :] <= position[:, None]) & (position[:, None] < window_ends[None, :])
    return jnp.sum(jnp.where(within, begins[None, :], 0), 1)


def inside(first_row, row_pos, key_pos):
    return (first_row[:, None] <= key_pos[None, :]) & (key_pos[None, :] <= row_pos[:, None])


def absorb(softmax_state, queries, key_values, allowed):
    highest, denominator, weighted = softmax_state
    head_size = queries.shape[-1]
    scores = jnp.einsum(
        "rhd,nd->rhn", queries, key_values[:, :head_size], preferred_element_type=jnp.float32
    )
    scores = jnp.where(allowed[:, None, :], scores, -jnp.inf)
    updated = jnp.maximum(highest, jnp.max(scores, -1))
    rescale = jnp.exp(highest - updated)
    weights = jnp.exp(scores - updated[..., None])
    denominator = rescale * denominator + jnp.sum(weights, -1)
    weighted = rescale[..., None] * weighted + jnp.einsum(
        "rhn,nd->rhd",
        weights.astype(jnp.bfloat16),
        key_values[:, head_size:],
        preferred_element_type=jnp.float32,
    )
    return (updated, denominator, weighted)


def absorb_sliced(softmax_state, queries, key_values, allowed):
    key_count = key_values.shape[0]
    piece = slice_blocks * BLOCK
    for begin in range(0, key_count, piece):
        finish = min(begin + piece, key_count)
        softmax_state = absorb(
            softmax_state, queries, key_values[begin:finish], allowed[:, begin:finish]
        )
    return softmax_state


def select(layout, wanted, total_blocks):
    blocks_dev = layout.shape[0]
    clipped = jnp.clip(wanted, 0, total_blocks - 1)
    return layout[clipped % blocks_dev, clipped // blocks_dev]


def by_request(
    tokens,
    norm_gain,
    query_weight,
    key_weight,
    value_weight,
    window_lengths,
    is_caption,
    span_blocks,
):
    ranks = lax.axis_size("seq")
    device_rank = lax.axis_index("seq")
    features = lax.all_gather(tokens, "head", axis=1, tiled=True)
    local_rows = features.shape[0]
    blocks_dev = local_rows // BLOCK
    total_blocks = blocks_dev * ranks
    window = min(window_cap, total_blocks * BLOCK // 4)
    span_most = min(span_cap, total_blocks // 4)
    window_back = (window + BLOCK - 2) // BLOCK
    first_pos = device_rank * local_rows
    row_pos = first_pos + jnp.arange(local_rows, dtype=jnp.int32)
    normed = rms_normed(features, norm_gain)
    head_dev = query_weight.shape[1] // HD
    kv_index = lax.axis_index("head") * head_dev // (H // KV)
    queries = jnp.dot(normed, query_weight, preferred_element_type=jnp.float32).reshape(
        local_rows, head_dev, HD
    )
    queries = (rotate(queries, row_pos) * HD ** (-0.5)).astype(jnp.bfloat16)
    key_columns = lax.dynamic_slice_in_dim(key_weight, kv_index * HD, HD, 1)
    value_columns = lax.dynamic_slice_in_dim(value_weight, kv_index * HD, HD, 1)
    key_rows = jnp.dot(normed, key_columns, preferred_element_type=jnp.float32).reshape(
        local_rows, 1, HD
    )
    key_rows = rotate(key_rows, row_pos).reshape(local_rows, HD).astype(jnp.bfloat16)
    value_rows = jnp.dot(normed, value_columns, preferred_element_type=jnp.float32).astype(
        jnp.bfloat16
    )
    key_values = jnp.concatenate([key_rows, value_rows], 1)
    window_first = window_starts(window_lengths, row_pos)
    caption_rows = is_caption == 1
    row_block = jnp.arange(local_rows, dtype=jnp.int32) // BLOCK
    span_end = span_blocks[:, 1][row_block]
    all_spans = lax.all_gather(span_blocks, "seq", axis=0, tiled=True)
    pieces = key_values.reshape(blocks_dev, ranks, BLOCK // ranks, 2 * HD)
    layout = lax.all_to_all(pieces, "seq", split_axis=1, concat_axis=1, tiled=True)
    offsets = jnp.arange(span_most, dtype=jnp.int32)
    span_wanted = all_spans[:, 0].reshape(ranks, blocks_dev, 1) + offsets[None, None, :]
    span_wanted = span_wanted.reshape(ranks, blocks_dev * span_most).T
    own_starts = span_blocks[:, 0]
    span_pos = (
        (own_starts[:, None] + offsets[None, :])[:, :, None] * BLOCK
        + jnp.arange(BLOCK, dtype=jnp.int32)[None, None, :]
    ).reshape(-1)
    span_owner = jnp.arange(blocks_dev * span_most * BLOCK, dtype=jnp.int32) // (span_most * BLOCK)
    span_ok = (span_owner[None, :] == row_block[:, None]) & (
        span_pos[None, :] // BLOCK <= span_end[:, None]
    )
    span_ok = span_ok & caption_rows[:, None] & ~inside(window_first, row_pos, span_pos)
    start_state = (
        jnp.full((local_rows, head_dev), lowest_start, jnp.float32),
        jnp.zeros((local_rows, head_dev), jnp.float32),
        jnp.zeros((local_rows, head_dev, HD), jnp.float32),
    )
    near_index = jnp.arange(window_back + blocks_dev, dtype=jnp.int32)
    near_wanted = (
        (jnp.arange(ranks, dtype=jnp.int32) * blocks_dev)[None, :]
        - window_back
        + near_index[:, None]
    )
    wanted = jnp.concatenate([near_wanted, span_wanted], 0)
    delivered = lax.all_to_all(
        select(layout, wanted, total_blocks), "seq", split_axis=1, concat_axis=1, tiled=True
    )
    gathered = delivered.reshape(-1, 2 * HD)
    near_pos = (first_pos // BLOCK - window_back) * BLOCK + jnp.arange(
        (window_back + blocks_dev) * BLOCK, dtype=jnp.int32
    )
    allowed = jnp.concatenate([inside(window_first, row_pos, near_pos), span_ok], 1)
    softmax_state = absorb_sliced(start_state, queries, gathered, allowed)
    highest, denominator, weighted = softmax_state
    return (
        (weighted / denominator[..., None]).reshape(local_rows, head_dev * HD).astype(jnp.bfloat16)
    )


def vmem(count):
    return [pl.BlockSpec(memory_space=pltpu.VMEM)] * count


def smem(count):
    return [pl.BlockSpec(memory_space=pltpu.SMEM)] * count


def turn(u, cosine, sine):
    return u * cosine + pltpu.roll(u, u.shape[-1] // 2, 1) * sine


def kv_kernel(
    place, x0, x1, x2, x3, gain, key_weight, value_weight, cosine, sine, kv_out, normed_out
):
    depth = x0.shape[1]
    parts = (x0, x1, x2, x3)
    me, kv_col = place[0], pl.multiple_of(place[1], HD)
    total = None
    for part in parts:
        hidden = part[...].astype(jnp.float32)
        squares = jnp.sum(hidden * hidden, -1, keepdims=True)
        total = squares if total is None else total + squares
    scale = lax.rsqrt(total / (depth * len(parts)) + norm_eps)
    keys = values = None
    for order, part in enumerate(parts):
        first = pl.multiple_of(jnp.bitwise_xor(me, order) * depth, depth)
        span = pl.ds(first, depth)
        normed = (part[...].astype(jnp.float32) * scale * gain[:, span]).astype(jnp.bfloat16)
        normed_out[:, span] = normed
        k = jnp.dot(
            normed, key_weight[span, pl.ds(kv_col, HD)], preferred_element_type=jnp.float32
        )
        v = jnp.dot(
            normed, value_weight[span, pl.ds(kv_col, HD)], preferred_element_type=jnp.float32
        )
        keys = k if keys is None else keys + k
        values = v if values is None else values + v
    kv_out[:, :HD] = turn(keys, cosine[...], sine[...]).astype(jnp.bfloat16)
    kv_out[:, HD:] = values.astype(jnp.bfloat16)


def query_kernel(normed, weight, cosine, sine, out):
    q = jnp.dot(normed[...], weight[...], preferred_element_type=jnp.float32)
    for begin in range(0, q.shape[1], HD):
        turned = turn(q[:, begin : begin + HD], cosine[...], sine[...])
        out[:, begin : begin + HD] = (turned * HD ** (-0.5)).astype(jnp.bfloat16)


def attend_kernel(blocks, place, lengths, spans, q, caption, *refs):
    kv, (out, scores, bias) = refs[:blocks], refs[blocks:]
    rows = q.shape[0]
    rank = place[0]
    row_pos = rank * rows + lax.broadcasted_iota(jnp.int32, (rows, BLOCK), 0)
    first_row = jnp.zeros((rows, BLOCK), jnp.int32)
    begin = jnp.int32(0)
    for w in range(lengths.shape[0]):
        end = begin + lengths[w]
        within = (row_pos >= begin) & (row_pos < end)
        first_row = jnp.where(within, begin, first_row)
        begin = end
    is_caption = jnp.broadcast_to(caption[...], (rows, BLOCK)) == 1
    for order in range(blocks):
        block = jnp.bitwise_xor(rank, order)
        key_pos = block * BLOCK + lax.broadcasted_iota(jnp.int32, (rows, BLOCK), 1)
        near = (first_row <= key_pos) & (key_pos <= row_pos)
        reached = (spans[0, 0] <= block) & (block <= spans[0, 1])
        allowed = near | (is_caption & reached)
        bias[:, order * BLOCK : (order + 1) * BLOCK] = jnp.where(allowed, 0.0, -jnp.inf)
    for head in range(q.shape[1] // HD):
        qh = q[:, head * HD : (head + 1) * HD]
        for order in range(blocks):
            columns = slice(order * BLOCK, (order + 1) * BLOCK)
            scores[:, columns] = (
                lax.dot_general(
                    qh,
                    kv[order][:, :HD],
                    (((1,), (1,)), ((), ())),
                    preferred_element_type=jnp.float32,
                )
                + bias[:, columns]
            )
        s = scores[...]
        highest = jnp.max(s, -1, keepdims=True)
        weights = jnp.exp(s - highest)
        denominator = jnp.sum(weights, -1, keepdims=True)
        rounded = weights.astype(jnp.bfloat16)
        mixed = None
        for order in range(blocks):
            part = jnp.dot(
                rounded[:, order * BLOCK : (order + 1) * BLOCK],
                kv[order][:, HD:],
                preferred_element_type=jnp.float32,
            )
            mixed = part if mixed is None else mixed + part
        out[:, head * HD : (head + 1) * HD] = (mixed / denominator).astype(jnp.bfloat16)


def everywhere(
    tokens,
    norm_gain,
    query_weight,
    key_weight,
    value_weight,
    window_lengths,
    is_caption,
    span_blocks,
):
    ranks, groups = lax.axis_size("seq"), lax.axis_size("head")
    rank, group = lax.axis_index("seq"), lax.axis_index("head")
    rows = tokens.shape[0]
    head_dev = query_weight.shape[1] // HD

    def pairs(shift):
        return [
            (r * groups + g, (r ^ shift(g)[0]) * groups + (g ^ shift(g)[1]))
            for r in range(ranks)
            for g in range(groups)
        ]

    def move(array, shift):
        return lax.ppermute(array, ("seq", "head"), pairs(shift))

    across = move(tokens, lambda g: (0, 2))
    beside = move(tokens, lambda g: (0, 1))
    half = HD // 2
    frequency = rope_base ** (-jnp.arange(half, dtype=jnp.float32) * 2.0 / HD)
    row_pos = rank * rows + jnp.arange(rows, dtype=jnp.int32)
    angles = row_pos.astype(jnp.float32)[:, None] * frequency[None, :]
    cosine = jnp.tile(jnp.cos(angles), (1, 2))
    sine = jnp.sin(angles)
    sine = jnp.concatenate([-sine, sine], 1)
    corner = move(across, lambda g: (0, 1))

    kv_index = group * head_dev // (H // KV)
    key_values, normed = pl.pallas_call(
        kv_kernel,
        out_shape=(
            jax.ShapeDtypeStruct((rows, 2 * HD), jnp.bfloat16),
            jax.ShapeDtypeStruct((rows, query_weight.shape[0]), jnp.bfloat16),
        ),
        in_specs=smem(1) + vmem(9),
        out_specs=tuple(vmem(2)),
        name="keys_values",
    )(
        jnp.stack([group, kv_index * HD]),
        tokens,
        beside,
        across,
        corner,
        norm_gain[None, :],
        key_weight,
        value_weight,
        cosine,
        sine,
    )

    blocks = {0: key_values}
    far = ranks // 2
    plan = [(far, far | 2), (far | 1, far | 3), (2, 1)]
    fetched = [
        (both, move(key_values, lambda g, both=both: (both[g % 2], 0))) for both in plan
    ]
    last = move(key_values, lambda g: (3, 0))
    queries = pl.pallas_call(
        query_kernel,
        out_shape=jax.ShapeDtypeStruct((rows, head_dev * HD), jnp.bfloat16),
        in_specs=vmem(4),
        out_specs=vmem(1)[0],
        name="queries",
    )(normed, query_weight, cosine, sine)
    odd = group % 2 == 1
    held = {0: key_values, 3: last}
    for both, own in fetched:
        other = move(own, lambda g: (0, 1))
        held[both[0]] = jnp.where(odd, other, own)
        held[both[1]] = jnp.where(odd, own, other)
    return pl.pallas_call(
        functools.partial(attend_kernel, ranks),
        out_shape=jax.ShapeDtypeStruct((rows, head_dev * HD), jnp.bfloat16),
        in_specs=smem(3) + vmem(2 + ranks),
        out_specs=vmem(1)[0],
        scratch_shapes=[
            pltpu.VMEM((rows, ranks * BLOCK), jnp.float32),
            pltpu.VMEM((rows, ranks * BLOCK), jnp.float32),
        ],
        name="attend",
    )(
        rank[None],
        window_lengths,
        span_blocks,
        queries,
        is_caption[:, None],
        *[held[order] for order in range(ranks)],
    )


def solution(mesh):
    ranks, groups = mesh.shape["seq"], mesh.shape["head"]
    in_specs = (P("seq", "head"), P(), P(None, "head"), P(), P(), P(), P("seq"), P("seq", None))
    out_specs = P("seq", "head")

    def per_device(*arguments):
        rows = arguments[0].shape[0]
        head_dev = arguments[2].shape[1] // HD
        shared = (H // KV) % (2 * head_dev) == 0
        whole = ranks == 8 and groups == 4 and rows == BLOCK and shared
        return (everywhere if whole else by_request)(*arguments)

    return jax.shard_map(
        per_device, mesh=mesh, in_specs=in_specs, out_specs=out_specs, check_vma=False
    )
```

```python
import functools

import jax
import jax.numpy as jnp
from jax import lax
from jax.experimental import pallas as pl
from jax.experimental.pallas import tpu as pltpu
from jax.sharding import PartitionSpec as P

H = 16
KV = 2
HD = 128
BLOCK = 128


norm_eps = 1e-05
rope_base = 500000.0
window_cap = 4096
span_cap = 8
slice_blocks = 8
lowest_start = -1e30


def rotate(vectors, position):
    half_size = vectors.shape[-1] // 2
    frequency = rope_base ** (-jnp.arange(half_size, dtype=jnp.float32) * 2.0 / vectors.shape[-1])
    angles = position.astype(jnp.float32)[:, None] * frequency[None, :]
    cosine = jnp.cos(angles)[:, None, :]
    sine_part = jnp.sin(angles)[:, None, :]
    first_half = vectors[..., :half_size]
    second_half = vectors[..., half_size:]
    return jnp.concatenate(
        [
            first_half * cosine - second_half * sine_part,
            second_half * cosine + first_half * sine_part,
        ],
        -1,
    )


def rms_normed(tokens, norm_gain):
    hidden = tokens.astype(jnp.float32)
    scale = lax.rsqrt(jnp.mean(hidden * hidden, -1, keepdims=True) + norm_eps)
    return (hidden * scale * norm_gain[None, :]).astype(jnp.bfloat16)


def window_starts(window_lengths, position):
    window_ends = jnp.cumsum(window_lengths)
    begins = window_ends - window_lengths
    within = (begins[None, :] <= position[:, None]) & (position[:, None] < window_ends[None, :])
    return jnp.sum(jnp.where(within, begins[None, :], 0), 1)


def inside(first_row, row_pos, key_pos):
    return (first_row[:, None] <= key_pos[None, :]) & (key_pos[None, :] <= row_pos[:, None])


def absorb(softmax_state, queries, key_values, allowed):
    highest, denominator, weighted = softmax_state
    head_size = queries.shape[-1]
    scores = jnp.einsum(
        "rhd,nd->rhn", queries, key_values[:, :head_size], preferred_element_type=jnp.float32
    )
    scores = jnp.where(allowed[:, None, :], scores, -jnp.inf)
    updated = jnp.maximum(highest, jnp.max(scores, -1))
    rescale = jnp.exp(highest - updated)
    weights = jnp.exp(scores - updated[..., None])
    denominator = rescale * denominator + jnp.sum(weights, -1)
    weighted = rescale[..., None] * weighted + jnp.einsum(
        "rhn,nd->rhd",
        weights.astype(jnp.bfloat16),
        key_values[:, head_size:],
        preferred_element_type=jnp.float32,
    )
    return (updated, denominator, weighted)


def absorb_sliced(softmax_state, queries, key_values, allowed):
    key_count = key_values.shape[0]
    piece = slice_blocks * BLOCK
    for begin in range(0, key_count, piece):
        finish = min(begin + piece, key_count)
        softmax_state = absorb(
            softmax_state, queries, key_values[begin:finish], allowed[:, begin:finish]
        )
    return softmax_state


def select(layout, wanted, total_blocks):
    blocks_dev = layout.shape[0]
    clipped = jnp.clip(wanted, 0, total_blocks - 1)
    return layout[clipped % blocks_dev, clipped // blocks_dev]


def by_request(
    tokens,
    norm_gain,
    query_weight,
    key_weight,
    value_weight,
    window_lengths,
    is_caption,
    span_blocks,
):
    ranks = lax.axis_size("seq")
    device_rank = lax.axis_index("seq")
    features = lax.all_gather(tokens, "head", axis=1, tiled=True)
    local_rows = features.shape[0]
    blocks_dev = local_rows // BLOCK
    total_blocks = blocks_dev * ranks
    window = min(window_cap, total_blocks * BLOCK // 4)
    span_most = min(span_cap, total_blocks // 4)
    window_back = (window + BLOCK - 2) // BLOCK
    first_pos = device_rank * local_rows
    row_pos = first_pos + jnp.arange(local_rows, dtype=jnp.int32)
    normed = rms_normed(features, norm_gain)
    head_dev = query_weight.shape[1] // HD
    kv_index = lax.axis_index("head") * head_dev // (H // KV)
    queries = jnp.dot(normed, query_weight, preferred_element_type=jnp.float32).reshape(
        local_rows, head_dev, HD
    )
    queries = (rotate(queries, row_pos) * HD ** (-0.5)).astype(jnp.bfloat16)
    key_columns = lax.dynamic_slice_in_dim(key_weight, kv_index * HD, HD, 1)
    value_columns = lax.dynamic_slice_in_dim(value_weight, kv_index * HD, HD, 1)
    key_rows = jnp.dot(normed, key_columns, preferred_element_type=jnp.float32).reshape(
        local_rows, 1, HD
    )
    key_rows = rotate(key_rows, row_pos).reshape(local_rows, HD).astype(jnp.bfloat16)
    value_rows = jnp.dot(normed, value_columns, preferred_element_type=jnp.float32).astype(
        jnp.bfloat16
    )
    key_values = jnp.concatenate([key_rows, value_rows], 1)
    window_first = window_starts(window_lengths, row_pos)
    caption_rows = is_caption == 1
    row_block = jnp.arange(local_rows, dtype=jnp.int32) // BLOCK
    span_end = span_blocks[:, 1][row_block]
    all_spans = lax.all_gather(span_blocks, "seq", axis=0, tiled=True)
    pieces = key_values.reshape(blocks_dev, ranks, BLOCK // ranks, 2 * HD)
    layout = lax.all_to_all(pieces, "seq", split_axis=1, concat_axis=1, tiled=True)
    offsets = jnp.arange(span_most, dtype=jnp.int32)
    span_wanted = all_spans[:, 0].reshape(ranks, blocks_dev, 1) + offsets[None, None, :]
    span_wanted = span_wanted.reshape(ranks, blocks_dev * span_most).T
    own_starts = span_blocks[:, 0]
    span_pos = (
        (own_starts[:, None] + offsets[None, :])[:, :, None] * BLOCK
        + jnp.arange(BLOCK, dtype=jnp.int32)[None, None, :]
    ).reshape(-1)
    span_owner = jnp.arange(blocks_dev * span_most * BLOCK, dtype=jnp.int32) // (span_most * BLOCK)
    span_ok = (span_owner[None, :] == row_block[:, None]) & (
        span_pos[None, :] // BLOCK <= span_end[:, None]
    )
    span_ok = span_ok & caption_rows[:, None] & ~inside(window_first, row_pos, span_pos)
    start_state = (
        jnp.full((local_rows, head_dev), lowest_start, jnp.float32),
        jnp.zeros((local_rows, head_dev), jnp.float32),
        jnp.zeros((local_rows, head_dev, HD), jnp.float32),
    )
    near_index = jnp.arange(window_back + blocks_dev, dtype=jnp.int32)
    near_wanted = (
        (jnp.arange(ranks, dtype=jnp.int32) * blocks_dev)[None, :]
        - window_back
        + near_index[:, None]
    )
    wanted = jnp.concatenate([near_wanted, span_wanted], 0)
    delivered = lax.all_to_all(
        select(layout, wanted, total_blocks), "seq", split_axis=1, concat_axis=1, tiled=True
    )
    gathered = delivered.reshape(-1, 2 * HD)
    near_pos = (first_pos // BLOCK - window_back) * BLOCK + jnp.arange(
        (window_back + blocks_dev) * BLOCK, dtype=jnp.int32
    )
    allowed = jnp.concatenate([inside(window_first, row_pos, near_pos), span_ok], 1)
    softmax_state = absorb_sliced(start_state, queries, gathered, allowed)
    highest, denominator, weighted = softmax_state
    return (
        (weighted / denominator[..., None]).reshape(local_rows, head_dev * HD).astype(jnp.bfloat16)
    )


def vmem(count):
    return [pl.BlockSpec(memory_space=pltpu.VMEM)] * count


def smem(count):
    return [pl.BlockSpec(memory_space=pltpu.SMEM)] * count


def grant(mebibytes):
    return pltpu.CompilerParams(vmem_limit_bytes=mebibytes << 20)


def near_core(array):
    return pltpu.with_memory_space_constraint(array, pltpu.VMEM)


def turn(u, cosine, sine):
    return u * cosine + pltpu.roll(u, u.shape[-1] // 2, 1) * sine


def tables(cosine, sine):
    c, s = cosine[...], sine[...]
    return jnp.concatenate([c, c], 1), jnp.concatenate([-s, s], 1)


def load_kernel(sharers, tokens, gain, key_weight, value_weight, query_weight, caption, *refs):
    outs, sems = refs[:-1], refs[-1]
    tokens_out, gain_out, weight_out, query_out, caption_out = outs
    column = pl.multiple_of(lax.axis_index("head") // sharers * HD, HD)
    pairs = (
        (key_weight.at[:, pl.ds(column, HD)], weight_out.at[:, :HD]),
        (value_weight.at[:, pl.ds(column, HD)], weight_out.at[:, HD:]),
        (tokens, tokens_out),
        (gain, gain_out),
        (caption, caption_out),
        (query_weight, query_out),
    )
    copies = [pltpu.make_async_copy(a, b, sems.at[i]) for i, (a, b) in enumerate(pairs)]
    for copy in copies:
        copy.start()
    for copy in copies:
        copy.wait()


def kv_kernel(x0, x1, x2, x3, gain, weight, cosine, sine, kv_out, normed_out):
    depth = x0.shape[1]
    parts = (x0, x1, x2, x3)
    me = lax.axis_index("head")
    total = None
    for part in parts:
        hidden = part[...].astype(jnp.float32)
        squares = jnp.sum(hidden * hidden, -1, keepdims=True)
        total = squares if total is None else total + squares
    scale = lax.rsqrt(total / (depth * len(parts)) + norm_eps)
    both = None
    for order, part in enumerate(parts):
        first = pl.multiple_of(jnp.bitwise_xor(me, order) * depth, depth)
        span = pl.ds(first, depth)
        normed = (part[...].astype(jnp.float32) * scale * gain[:, span]).astype(jnp.bfloat16)
        normed_out[:, span] = normed
        product = jnp.dot(normed, weight[span, :], preferred_element_type=jnp.float32)
        both = product if both is None else both + product
    kv_out[:, :HD] = turn(both[:, :HD], *tables(cosine, sine)).astype(jnp.bfloat16)
    kv_out[:, HD:] = both[:, HD:].astype(jnp.bfloat16)


def query_kernel(normed, weight, cosine, sine, out):
    q = jnp.dot(normed[...], weight[...], preferred_element_type=jnp.float32)
    c, s = tables(cosine, sine)
    for begin in range(0, q.shape[1], HD):
        turned = turn(q[:, begin : begin + HD], c, s)
        out[:, begin : begin + HD] = (turned * HD ** (-0.5)).astype(jnp.bfloat16)


def attend_kernel(offsets, lengths, spans, q, caption, *refs):
    blocks = len(offsets)
    kv, (out, scores, bias) = refs[:blocks], refs[blocks:]
    rows = q.shape[0]
    rank, odd = lax.axis_index("seq"), lax.rem(lax.axis_index("head"), 2)
    row_pos = rank * rows + lax.broadcasted_iota(jnp.int32, (rows, BLOCK), 0)
    first_row = jnp.zeros((rows, BLOCK), jnp.int32)
    begin = jnp.int32(0)
    for w in range(lengths.shape[0]):
        end = begin + lengths[w]
        within = (row_pos >= begin) & (row_pos < end)
        first_row = jnp.where(within, begin, first_row)
        begin = end
    is_caption = jnp.broadcast_to(caption[...], (rows, rows)).T == 1
    for order, (even_offset, odd_offset) in enumerate(offsets):
        offset = even_offset + odd * (odd_offset - even_offset)
        block = jnp.bitwise_xor(rank, offset)
        key_pos = block * BLOCK + lax.broadcasted_iota(jnp.int32, (rows, BLOCK), 1)
        near = (first_row <= key_pos) & (key_pos <= row_pos)
        reached = (spans[0, 0] <= block) & (block <= spans[0, 1])
        allowed = near | (is_caption & reached)
        bias[:, order * BLOCK : (order + 1) * BLOCK] = jnp.where(allowed, 0.0, -jnp.inf)
    for head in range(q.shape[1] // HD):
        qh = q[:, head * HD : (head + 1) * HD]
        for order in range(blocks):
            columns = slice(order * BLOCK, (order + 1) * BLOCK)
            scores[:, columns] = (
                lax.dot_general(
                    qh,
                    kv[order][:, :HD],
                    (((1,), (1,)), ((), ())),
                    preferred_element_type=jnp.float32,
                )
                + bias[:, columns]
            )
        s = scores[...]
        highest = jnp.max(s, -1, keepdims=True)
        weights = jnp.exp(s - highest)
        denominator = jnp.sum(weights, -1, keepdims=True)
        rounded = weights.astype(jnp.bfloat16)
        mixed = None
        for order in range(blocks):
            part = jnp.dot(
                rounded[:, order * BLOCK : (order + 1) * BLOCK],
                kv[order][:, HD:],
                preferred_element_type=jnp.float32,
            )
            mixed = part if mixed is None else mixed + part
        out[:, head * HD : (head + 1) * HD] = (mixed / denominator).astype(jnp.bfloat16)


def everywhere(
    tokens,
    norm_gain,
    query_weight,
    key_weight,
    value_weight,
    window_lengths,
    is_caption,
    span_blocks,
):
    ranks, groups = lax.axis_size("seq"), lax.axis_size("head")
    rank = lax.axis_index("seq")
    rows = tokens.shape[0]
    head_dev = query_weight.shape[1] // HD

    def move(array, shift):
        pairs = [
            (r * groups + g, (r ^ shift(g)[0]) * groups + (g ^ shift(g)[1]))
            for r in range(ranks)
            for g in range(groups)
        ]
        return lax.ppermute(array, ("seq", "head"), pairs)

    across = move(tokens, lambda g: (0, 2))
    beside = move(tokens, lambda g: (0, 1))
    features = query_weight.shape[0]
    row, gain, kv_weight, wide, captions = pl.pallas_call(
        functools.partial(load_kernel, H // KV // head_dev),
        out_shape=(
            pltpu.VMEM(tokens.shape, tokens.dtype),
            pltpu.VMEM((1, features), norm_gain.dtype),
            pltpu.VMEM((features, 2 * HD), key_weight.dtype),
            pltpu.VMEM(query_weight.shape, query_weight.dtype),
            pltpu.VMEM((1, rows), is_caption.dtype),
        ),
        in_specs=[pl.BlockSpec(memory_space=pltpu.HBM)] * 6,
        out_specs=tuple(vmem(5)),
        scratch_shapes=[pltpu.SemaphoreType.DMA((6,))],
        compiler_params=grant(2),
        name="load",
    )(
        *[
            pltpu.with_memory_space_constraint(array, pltpu.HBM)
            for array in (
                tokens,
                norm_gain[None, :],
                key_weight,
                value_weight,
                query_weight,
                is_caption[None, :],
            )
        ]
    )
    half = HD // 2
    frequency = rope_base ** (-jnp.arange(half, dtype=jnp.float32) * 2.0 / HD)
    row_pos = rank * rows + jnp.arange(rows, dtype=jnp.int32)
    angles = row_pos.astype(jnp.float32)[:, None] * frequency[None, :]
    cosine, sine = near_core(jnp.cos(angles)), near_core(jnp.sin(angles))
    corner = move(across, lambda g: (0, 1))

    key_values, normed = pl.pallas_call(
        kv_kernel,
        out_shape=(
            pltpu.VMEM((rows, 2 * HD), jnp.bfloat16),
            pltpu.VMEM((rows, features), jnp.bfloat16),
        ),
        in_specs=vmem(8),
        out_specs=tuple(vmem(2)),
        compiler_params=grant(6),
        name="keys_values",
    )(
        near_core(row),
        near_core(beside),
        near_core(across),
        near_core(corner),
        near_core(gain),
        near_core(kv_weight),
        cosine,
        sine,
    )

    far = ranks // 2
    plan = [(far, far | 2), (far | 1, far | 3), (2, 1)]
    fetched = [move(key_values, lambda g, both=both: (both[g % 2], 0)) for both in plan]
    last = move(key_values, lambda g: (3, 0))
    queries = pl.pallas_call(
        query_kernel,
        out_shape=pltpu.VMEM((rows, head_dev * HD), jnp.bfloat16),
        in_specs=vmem(4),
        out_specs=vmem(1)[0],
        compiler_params=grant(4),
        name="queries",
    )(near_core(normed), near_core(wide), cosine, sine)
    offsets, held = [(0, 0), (3, 3)], [key_values, last]
    for both, own in zip(plan, fetched):
        offsets += [both, both[::-1]]
        held += [own, move(own, lambda g: (0, 1))]
    return pl.pallas_call(
        functools.partial(attend_kernel, offsets),
        out_shape=jax.ShapeDtypeStruct((rows, head_dev * HD), jnp.bfloat16),
        in_specs=smem(2) + vmem(2 + ranks),
        out_specs=vmem(1)[0],
        scratch_shapes=[
            pltpu.VMEM((rows, ranks * BLOCK), jnp.float32),
            pltpu.VMEM((rows, ranks * BLOCK), jnp.float32),
        ],
        compiler_params=grant(8),
        name="attend",
    )(
        window_lengths,
        span_blocks,
        near_core(queries),
        near_core(captions),
        *[near_core(array) for array in held],
    )


def solution(mesh):
    ranks, groups = mesh.shape["seq"], mesh.shape["head"]
    in_specs = (P("seq", "head"), P(), P(None, "head"), P(), P(), P(), P("seq"), P("seq", None))
    out_specs = P("seq", "head")

    def per_device(*arguments):
        rows = arguments[0].shape[0]
        head_dev = arguments[2].shape[1] // HD
        shared = (H // KV) % (2 * head_dev) == 0
        whole = ranks == 8 and groups == 4 and rows == BLOCK and shared
        return (everywhere if whole else by_request)(*arguments)

    return jax.shard_map(
        per_device, mesh=mesh, in_specs=in_specs, out_specs=out_specs, check_vma=False
    )
```

```python
import functools

import jax
import jax.numpy as jnp
from jax import lax
from jax.experimental import pallas as pl
from jax.experimental.pallas import tpu as pltpu
from jax.sharding import PartitionSpec as P

H = 16
KV = 2
HD = 128
BLOCK = 128


norm_eps = 1e-05
rope_base = 500000.0
window_cap = 4096
span_cap = 8
slice_blocks = 8
lowest_start = -1e30


def rotate(vectors, position):
    half_size = vectors.shape[-1] // 2
    frequency = rope_base ** (-jnp.arange(half_size, dtype=jnp.float32) * 2.0 / vectors.shape[-1])
    angles = position.astype(jnp.float32)[:, None] * frequency[None, :]
    cosine = jnp.cos(angles)[:, None, :]
    sine_part = jnp.sin(angles)[:, None, :]
    first_half = vectors[..., :half_size]
    second_half = vectors[..., half_size:]
    return jnp.concatenate(
        [
            first_half * cosine - second_half * sine_part,
            second_half * cosine + first_half * sine_part,
        ],
        -1,
    )


def rms_normed(tokens, norm_gain):
    hidden = tokens.astype(jnp.float32)
    scale = lax.rsqrt(jnp.mean(hidden * hidden, -1, keepdims=True) + norm_eps)
    return (hidden * scale * norm_gain[None, :]).astype(jnp.bfloat16)


def window_starts(window_lengths, position):
    window_ends = jnp.cumsum(window_lengths)
    begins = window_ends - window_lengths
    within = (begins[None, :] <= position[:, None]) & (position[:, None] < window_ends[None, :])
    return jnp.sum(jnp.where(within, begins[None, :], 0), 1)


def inside(first_row, row_pos, key_pos):
    return (first_row[:, None] <= key_pos[None, :]) & (key_pos[None, :] <= row_pos[:, None])


def absorb(softmax_state, queries, key_values, allowed):
    highest, denominator, weighted = softmax_state
    head_size = queries.shape[-1]
    scores = jnp.einsum(
        "rhd,nd->rhn", queries, key_values[:, :head_size], preferred_element_type=jnp.float32
    )
    scores = jnp.where(allowed[:, None, :], scores, -jnp.inf)
    updated = jnp.maximum(highest, jnp.max(scores, -1))
    rescale = jnp.exp(highest - updated)
    weights = jnp.exp(scores - updated[..., None])
    denominator = rescale * denominator + jnp.sum(weights, -1)
    weighted = rescale[..., None] * weighted + jnp.einsum(
        "rhn,nd->rhd",
        weights.astype(jnp.bfloat16),
        key_values[:, head_size:],
        preferred_element_type=jnp.float32,
    )
    return (updated, denominator, weighted)


def absorb_sliced(softmax_state, queries, key_values, allowed):
    key_count = key_values.shape[0]
    piece = slice_blocks * BLOCK
    for begin in range(0, key_count, piece):
        finish = min(begin + piece, key_count)
        softmax_state = absorb(
            softmax_state, queries, key_values[begin:finish], allowed[:, begin:finish]
        )
    return softmax_state


def select(layout, wanted, total_blocks):
    blocks_dev = layout.shape[0]
    clipped = jnp.clip(wanted, 0, total_blocks - 1)
    return layout[clipped % blocks_dev, clipped // blocks_dev]


def by_request(
    tokens,
    norm_gain,
    query_weight,
    key_weight,
    value_weight,
    window_lengths,
    is_caption,
    span_blocks,
):
    ranks = lax.axis_size("seq")
    device_rank = lax.axis_index("seq")
    features = lax.all_gather(tokens, "head", axis=1, tiled=True)
    local_rows = features.shape[0]
    blocks_dev = local_rows // BLOCK
    total_blocks = blocks_dev * ranks
    window = min(window_cap, total_blocks * BLOCK // 4)
    span_most = min(span_cap, total_blocks // 4)
    window_back = (window + BLOCK - 2) // BLOCK
    first_pos = device_rank * local_rows
    row_pos = first_pos + jnp.arange(local_rows, dtype=jnp.int32)
    normed = rms_normed(features, norm_gain)
    head_dev = query_weight.shape[1] // HD
    kv_index = lax.axis_index("head") * head_dev // (H // KV)
    queries = jnp.dot(normed, query_weight, preferred_element_type=jnp.float32).reshape(
        local_rows, head_dev, HD
    )
    queries = (rotate(queries, row_pos) * HD ** (-0.5)).astype(jnp.bfloat16)
    key_columns = lax.dynamic_slice_in_dim(key_weight, kv_index * HD, HD, 1)
    value_columns = lax.dynamic_slice_in_dim(value_weight, kv_index * HD, HD, 1)
    key_rows = jnp.dot(normed, key_columns, preferred_element_type=jnp.float32).reshape(
        local_rows, 1, HD
    )
    key_rows = rotate(key_rows, row_pos).reshape(local_rows, HD).astype(jnp.bfloat16)
    value_rows = jnp.dot(normed, value_columns, preferred_element_type=jnp.float32).astype(
        jnp.bfloat16
    )
    key_values = jnp.concatenate([key_rows, value_rows], 1)
    window_first = window_starts(window_lengths, row_pos)
    caption_rows = is_caption == 1
    row_block = jnp.arange(local_rows, dtype=jnp.int32) // BLOCK
    span_end = span_blocks[:, 1][row_block]
    all_spans = lax.all_gather(span_blocks, "seq", axis=0, tiled=True)
    pieces = key_values.reshape(blocks_dev, ranks, BLOCK // ranks, 2 * HD)
    layout = lax.all_to_all(pieces, "seq", split_axis=1, concat_axis=1, tiled=True)
    offsets = jnp.arange(span_most, dtype=jnp.int32)
    span_wanted = all_spans[:, 0].reshape(ranks, blocks_dev, 1) + offsets[None, None, :]
    span_wanted = span_wanted.reshape(ranks, blocks_dev * span_most).T
    own_starts = span_blocks[:, 0]
    span_pos = (
        (own_starts[:, None] + offsets[None, :])[:, :, None] * BLOCK
        + jnp.arange(BLOCK, dtype=jnp.int32)[None, None, :]
    ).reshape(-1)
    span_owner = jnp.arange(blocks_dev * span_most * BLOCK, dtype=jnp.int32) // (span_most * BLOCK)
    span_ok = (span_owner[None, :] == row_block[:, None]) & (
        span_pos[None, :] // BLOCK <= span_end[:, None]
    )
    span_ok = span_ok & caption_rows[:, None] & ~inside(window_first, row_pos, span_pos)
    start_state = (
        jnp.full((local_rows, head_dev), lowest_start, jnp.float32),
        jnp.zeros((local_rows, head_dev), jnp.float32),
        jnp.zeros((local_rows, head_dev, HD), jnp.float32),
    )
    near_index = jnp.arange(window_back + blocks_dev, dtype=jnp.int32)
    near_wanted = (
        (jnp.arange(ranks, dtype=jnp.int32) * blocks_dev)[None, :]
        - window_back
        + near_index[:, None]
    )
    wanted = jnp.concatenate([near_wanted, span_wanted], 0)
    delivered = lax.all_to_all(
        select(layout, wanted, total_blocks), "seq", split_axis=1, concat_axis=1, tiled=True
    )
    gathered = delivered.reshape(-1, 2 * HD)
    near_pos = (first_pos // BLOCK - window_back) * BLOCK + jnp.arange(
        (window_back + blocks_dev) * BLOCK, dtype=jnp.int32
    )
    allowed = jnp.concatenate([inside(window_first, row_pos, near_pos), span_ok], 1)
    softmax_state = absorb_sliced(start_state, queries, gathered, allowed)
    _, denominator, weighted = softmax_state
    return (
        (weighted / denominator[..., None]).reshape(local_rows, head_dev * HD).astype(jnp.bfloat16)
    )


def vmem(count):
    return [pl.BlockSpec(memory_space=pltpu.VMEM)] * count


def smem(count):
    return [pl.BlockSpec(memory_space=pltpu.SMEM)] * count


def grant(mebibytes):
    return pltpu.CompilerParams(vmem_limit_bytes=mebibytes << 20)


def near_core(array):
    return pltpu.with_memory_space_constraint(array, pltpu.VMEM)


def turn(u, cosine, sine):
    return u * cosine + pltpu.roll(u, u.shape[-1] // 2, 1) * sine


def tables(cosine, sine):
    c, s = cosine[...], sine[...]
    return jnp.concatenate([c, c], 1), jnp.concatenate([-s, s], 1)


def load_kernel(sharers, tokens, gain, key_weight, value_weight, query_weight, caption, *refs):
    outs, sems = refs[:-1], refs[-1]
    tokens_out, gain_out, weight_out, query_out, caption_out = outs
    column = pl.multiple_of(lax.axis_index("head") // sharers * HD, HD)
    pairs = (
        (key_weight.at[:, pl.ds(column, HD)], weight_out.at[:, :HD]),
        (value_weight.at[:, pl.ds(column, HD)], weight_out.at[:, HD:]),
        (tokens, tokens_out),
        (gain, gain_out),
        (caption, caption_out),
        (query_weight, query_out),
    )
    copies = [pltpu.make_async_copy(a, b, sems.at[i]) for i, (a, b) in enumerate(pairs)]
    for copy in copies:
        copy.start()
    for copy in copies:
        copy.wait()


def kv_kernel(x0, x1, x2, x3, gain, weight, cosine, sine, kv_out, normed_out):
    depth = x0.shape[1]
    parts = (x0, x1, x2, x3)
    me = lax.axis_index("head")
    total = None
    for part in parts:
        hidden = part[...].astype(jnp.float32)
        squares = jnp.sum(hidden * hidden, -1, keepdims=True)
        total = squares if total is None else total + squares
    scale = lax.rsqrt(total / (depth * len(parts)) + norm_eps)
    both = None
    for order, part in enumerate(parts):
        first = pl.multiple_of(jnp.bitwise_xor(me, order) * depth, depth)
        span = pl.ds(first, depth)
        normed = (part[...].astype(jnp.float32) * scale * gain[:, span]).astype(jnp.bfloat16)
        normed_out[:, span] = normed
        product = jnp.dot(normed, weight[span, :], preferred_element_type=jnp.float32)
        both = product if both is None else both + product
    kv_out[:, :HD] = turn(both[:, :HD], *tables(cosine, sine)).astype(jnp.bfloat16)
    kv_out[:, HD:] = both[:, HD:].astype(jnp.bfloat16)


def block_of(offset):
    odd = lax.rem(lax.axis_index("head"), 2)
    return jnp.bitwise_xor(lax.axis_index("seq"), offset[0] + odd * (offset[1] - offset[0]))


def fold(q, bias, columns, kv, scores, rounded, old, new):
    rows = bias.shape[0]
    for i, block in enumerate(kv):
        scores[:, i * BLOCK : (i + 1) * BLOCK] = lax.dot_general(
            q[...],
            block[:, :HD],
            (((1,), (1,)), ((), ())),
            preferred_element_type=jnp.float32,
        )
    width = len(kv) * BLOCK
    for begin in range(0, q.shape[0], rows):
        part = slice(begin, begin + rows)
        s = scores[part, :width] + jnp.concatenate([bias[:, c : c + BLOCK] for c in columns], 1)
        highest = jnp.broadcast_to(jnp.max(s, -1, keepdims=True), (rows, BLOCK))
        if old is not None:
            highest = jnp.maximum(highest, old[0][part, :])
        total = None
        for i in range(len(kv)):
            piece = slice(i * BLOCK, (i + 1) * BLOCK)
            weights = jnp.exp(s[:, piece] - highest)
            rounded[part, piece] = weights.astype(jnp.bfloat16)
            total = weights if total is None else total + weights
        mixed = None
        for i, block in enumerate(kv):
            piece = slice(i * BLOCK, (i + 1) * BLOCK)
            product = jnp.dot(
                rounded[part, piece], block[:, HD:], preferred_element_type=jnp.float32
            )
            mixed = product if mixed is None else mixed + product
        if old is not None:
            rescale = jnp.exp(old[0][part, :] - highest)
            total = total + rescale * old[1][part, :]
            mixed = mixed + rescale * old[2][part, :]
        new(begin // rows, part, highest, total, mixed)


def keep(state):
    def new(_, part, *values):
        for ref, value in zip(state, values):
            ref[part, :] = value

    return new


def query_kernel(
    offsets, lengths, spans, normed, weight, cosine, sine, caption, own, *refs
):
    (q, bias), state, (scores, rounded) = refs[:2], refs[2:5], refs[5:]
    rows = normed.shape[0]
    rank = lax.axis_index("seq")
    product = jnp.dot(normed[...], weight[...], preferred_element_type=jnp.float32)
    c, s = tables(cosine, sine)
    for begin in range(0, product.shape[1], HD):
        turned = turn(product[:, begin : begin + HD], c, s)
        first = begin // HD * rows
        q[first : first + rows, :] = (turned * HD ** (-0.5)).astype(jnp.bfloat16)
    row_pos = rank * rows + lax.broadcasted_iota(jnp.int32, (rows, BLOCK), 0)
    first_row = jnp.zeros((rows, BLOCK), jnp.int32)
    begin = jnp.int32(0)
    for w in range(lengths.shape[0]):
        end = begin + lengths[w]
        within = (row_pos >= begin) & (row_pos < end)
        first_row = jnp.where(within, begin, first_row)
        begin = end
    is_caption = jnp.broadcast_to(caption[...], (rows, rows)).T == 1
    for order, offset in enumerate(offsets):
        block = block_of(offset)
        key_pos = block * BLOCK + lax.broadcasted_iota(jnp.int32, (rows, BLOCK), 1)
        near = (first_row <= key_pos) & (key_pos <= row_pos)
        reached = (spans[0, 0] <= block) & (block <= spans[0, 1])
        allowed = near | (is_caption & reached)
        bias[:, order * BLOCK : (order + 1) * BLOCK] = jnp.where(allowed, 0.0, -jnp.inf)
    fold(q, bias, [0], [own], scores, rounded, None, keep(state))


def middle_kernel(columns, q, bias, *refs):
    old, kv = refs[:3], refs[3 : 3 + len(columns)]
    state, (scores, rounded) = refs[3 + len(columns) : 6 + len(columns)], refs[6 + len(columns) :]
    fold(q, bias, columns, kv, scores, rounded, old, keep(state))


def last_kernel(columns, q, bias, *refs):
    old, kv = refs[:3], refs[3 : 3 + len(columns)]
    out, scores, rounded = refs[3 + len(columns) :]

    def new(head, _, highest, total, mixed):
        denominator = jnp.sum(total, -1, keepdims=True)
        out[:, head * HD : (head + 1) * HD] = (mixed / denominator).astype(jnp.bfloat16)

    fold(q, bias, columns, kv, scores, rounded, old, new)


def everywhere(
    tokens,
    norm_gain,
    query_weight,
    key_weight,
    value_weight,
    window_lengths,
    is_caption,
    span_blocks,
):
    ranks, groups = lax.axis_size("seq"), lax.axis_size("head")
    rank = lax.axis_index("seq")
    rows = tokens.shape[0]
    head_dev = query_weight.shape[1] // HD

    def move(array, shift):
        pairs = [
            (r * groups + g, (r ^ shift(g)[0]) * groups + (g ^ shift(g)[1]))
            for r in range(ranks)
            for g in range(groups)
        ]
        return lax.ppermute(array, ("seq", "head"), pairs)

    across = move(tokens, lambda g: (0, 2))
    beside = move(tokens, lambda g: (0, 1))
    features = query_weight.shape[0]
    row, gain, kv_weight, wide, captions = pl.pallas_call(
        functools.partial(load_kernel, H // KV // head_dev),
        out_shape=(
            pltpu.VMEM(tokens.shape, tokens.dtype),
            pltpu.VMEM((1, features), norm_gain.dtype),
            pltpu.VMEM((features, 2 * HD), key_weight.dtype),
            pltpu.VMEM(query_weight.shape, query_weight.dtype),
            pltpu.VMEM((1, rows), is_caption.dtype),
        ),
        in_specs=[pl.BlockSpec(memory_space=pltpu.HBM)] * 6,
        out_specs=tuple(vmem(5)),
        scratch_shapes=[pltpu.SemaphoreType.DMA((6,))],
        compiler_params=grant(2),
        name="load",
    )(
        *[
            pltpu.with_memory_space_constraint(array, pltpu.HBM)
            for array in (
                tokens,
                norm_gain[None, :],
                key_weight,
                value_weight,
                query_weight,
                is_caption[None, :],
            )
        ]
    )
    half = HD // 2
    frequency = rope_base ** (-jnp.arange(half, dtype=jnp.float32) * 2.0 / HD)
    row_pos = rank * rows + jnp.arange(rows, dtype=jnp.int32)
    angles = row_pos.astype(jnp.float32)[:, None] * frequency[None, :]
    cosine, sine = near_core(jnp.cos(angles)), near_core(jnp.sin(angles))
    corner = move(across, lambda g: (0, 1))

    key_values, normed = pl.pallas_call(
        kv_kernel,
        out_shape=(
            pltpu.VMEM((rows, 2 * HD), jnp.bfloat16),
            pltpu.VMEM((rows, features), jnp.bfloat16),
        ),
        in_specs=vmem(8),
        out_specs=tuple(vmem(2)),
        compiler_params=grant(6),
        name="keys_values",
    )(
        near_core(row),
        near_core(beside),
        near_core(across),
        near_core(corner),
        near_core(gain),
        near_core(kv_weight),
        cosine,
        sine,
    )

    far = ranks // 2
    tall = rows * head_dev

    def swapped(array):
        return move(array, lambda g: (0, 1))

    def split(array, both):
        return move(array, lambda g: (both[g % 2], 0))

    column = split(key_values, (far, far | 2))
    row = split(key_values, (2, 1))
    corner = split(key_values, (3, 3))
    diagonal = split(key_values, (far | 1, far | 3))
    held = [
        ((0, 0), key_values),
        ((2, 1), row),
        ((1, 2), swapped(row)),
        ((far, far | 2), column),
        ((far | 2, far), swapped(column)),
        ((3, 3), corner),
        ((far | 1, far | 3), diagonal),
        ((far | 3, far | 1), swapped(diagonal)),
    ]
    offsets, arrays = [offset for offset, _ in held], [near_core(array) for _, array in held]
    state = [pltpu.VMEM((tall, BLOCK), jnp.float32)] * 2 + [pltpu.VMEM((tall, HD), jnp.float32)]

    def work(count):
        return [
            pltpu.VMEM((tall, count * BLOCK), jnp.float32),
            pltpu.VMEM((tall, count * BLOCK), jnp.bfloat16),
        ]

    q, bias, *partial = pl.pallas_call(
        functools.partial(query_kernel, offsets),
        out_shape=(
            pltpu.VMEM((tall, HD), jnp.bfloat16),
            pltpu.VMEM((rows, ranks * BLOCK), jnp.float32),
            *state,
        ),
        in_specs=smem(2) + vmem(6),
        out_specs=tuple(vmem(5)),
        scratch_shapes=work(1),
        compiler_params=grant(6),
        name="queries",
    )(
        window_lengths,
        span_blocks,
        near_core(normed),
        near_core(wide),
        cosine,
        sine,
        near_core(captions),
        arrays[0],
    )

    def columns(first, end):
        return [order * BLOCK for order in range(first, end)]

    later = ranks - 3
    partial = pl.pallas_call(
        functools.partial(middle_kernel, columns(1, later)),
        out_shape=tuple(state),
        in_specs=vmem(5 + later - 1),
        out_specs=tuple(vmem(3)),
        scratch_shapes=work(later - 1),
        compiler_params=grant(6),
        name="middle",
    )(*[near_core(array) for array in (q, bias, *partial)], *arrays[1:later])
    return pl.pallas_call(
        functools.partial(last_kernel, columns(later, ranks)),
        out_shape=jax.ShapeDtypeStruct((rows, head_dev * HD), jnp.bfloat16),
        in_specs=vmem(5 + ranks - later),
        out_specs=vmem(1)[0],
        scratch_shapes=work(ranks - later),
        compiler_params=grant(6),
        name="last",
    )(*[near_core(array) for array in (q, bias, *partial)], *arrays[later:])


def solution(mesh):
    ranks, groups = mesh.shape["seq"], mesh.shape["head"]
    in_specs = (P("seq", "head"), P(), P(None, "head"), P(), P(), P(), P("seq"), P("seq", None))
    out_specs = P("seq", "head")

    def per_device(*arguments):
        rows = arguments[0].shape[0]
        head_dev = arguments[2].shape[1] // HD
        shared = (H // KV) % (2 * head_dev) == 0
        whole = ranks == 8 and groups == 4 and rows == BLOCK and shared
        return (everywhere if whole else by_request)(*arguments)

    return jax.shard_map(
        per_device, mesh=mesh, in_specs=in_specs, out_specs=out_specs, check_vma=False
    )
```

```python
import functools

import jax
import jax.numpy as jnp
from jax import lax
from jax.experimental import pallas as pl
from jax.experimental.pallas import tpu as pltpu
from jax.sharding import PartitionSpec as P

H = 16
KV = 2
HD = 128
BLOCK = 128


norm_eps = 1e-05
rope_base = 500000.0
window_cap = 4096
span_cap = 8
slice_blocks = 8
lowest_start = -1e30


def rotate(vectors, position):
    half_size = vectors.shape[-1] // 2
    frequency = rope_base ** (-jnp.arange(half_size, dtype=jnp.float32) * 2.0 / vectors.shape[-1])
    angles = position.astype(jnp.float32)[:, None] * frequency[None, :]
    cosine = jnp.cos(angles)[:, None, :]
    sine_part = jnp.sin(angles)[:, None, :]
    first_half = vectors[..., :half_size]
    second_half = vectors[..., half_size:]
    return jnp.concatenate(
        [
            first_half * cosine - second_half * sine_part,
            second_half * cosine + first_half * sine_part,
        ],
        -1,
    )


def rms_normed(tokens, norm_gain):
    hidden = tokens.astype(jnp.float32)
    scale = lax.rsqrt(jnp.mean(hidden * hidden, -1, keepdims=True) + norm_eps)
    return (hidden * scale * norm_gain[None, :]).astype(jnp.bfloat16)


def window_starts(window_lengths, position):
    window_ends = jnp.cumsum(window_lengths)
    begins = window_ends - window_lengths
    within = (begins[None, :] <= position[:, None]) & (position[:, None] < window_ends[None, :])
    return jnp.sum(jnp.where(within, begins[None, :], 0), 1)


def inside(first_row, row_pos, key_pos):
    return (first_row[:, None] <= key_pos[None, :]) & (key_pos[None, :] <= row_pos[:, None])


def absorb(softmax_state, queries, key_values, allowed):
    highest, denominator, weighted = softmax_state
    head_size = queries.shape[-1]
    scores = jnp.einsum(
        "rhd,nd->rhn", queries, key_values[:, :head_size], preferred_element_type=jnp.float32
    )
    scores = jnp.where(allowed[:, None, :], scores, -jnp.inf)
    updated = jnp.maximum(highest, jnp.max(scores, -1))
    rescale = jnp.exp(highest - updated)
    weights = jnp.exp(scores - updated[..., None])
    denominator = rescale * denominator + jnp.sum(weights, -1)
    weighted = rescale[..., None] * weighted + jnp.einsum(
        "rhn,nd->rhd",
        weights.astype(jnp.bfloat16),
        key_values[:, head_size:],
        preferred_element_type=jnp.float32,
    )
    return (updated, denominator, weighted)


def absorb_sliced(softmax_state, queries, key_values, allowed):
    key_count = key_values.shape[0]
    piece = slice_blocks * BLOCK
    for begin in range(0, key_count, piece):
        finish = min(begin + piece, key_count)
        softmax_state = absorb(
            softmax_state, queries, key_values[begin:finish], allowed[:, begin:finish]
        )
    return softmax_state


def select(layout, wanted, total_blocks):
    blocks_dev = layout.shape[0]
    clipped = jnp.clip(wanted, 0, total_blocks - 1)
    return layout[clipped % blocks_dev, clipped // blocks_dev]


def by_request(
    tokens,
    norm_gain,
    query_weight,
    key_weight,
    value_weight,
    window_lengths,
    is_caption,
    span_blocks,
):
    ranks = lax.axis_size("seq")
    device_rank = lax.axis_index("seq")
    features = lax.all_gather(tokens, "head", axis=1, tiled=True)
    local_rows = features.shape[0]
    blocks_dev = local_rows // BLOCK
    total_blocks = blocks_dev * ranks
    window = min(window_cap, total_blocks * BLOCK // 4)
    span_most = min(span_cap, total_blocks // 4)
    window_back = (window + BLOCK - 2) // BLOCK
    first_pos = device_rank * local_rows
    row_pos = first_pos + jnp.arange(local_rows, dtype=jnp.int32)
    normed = rms_normed(features, norm_gain)
    head_dev = query_weight.shape[1] // HD
    kv_index = lax.axis_index("head") * head_dev // (H // KV)
    queries = jnp.dot(normed, query_weight, preferred_element_type=jnp.float32).reshape(
        local_rows, head_dev, HD
    )
    queries = (rotate(queries, row_pos) * HD ** (-0.5)).astype(jnp.bfloat16)
    key_columns = lax.dynamic_slice_in_dim(key_weight, kv_index * HD, HD, 1)
    value_columns = lax.dynamic_slice_in_dim(value_weight, kv_index * HD, HD, 1)
    key_rows = jnp.dot(normed, key_columns, preferred_element_type=jnp.float32).reshape(
        local_rows, 1, HD
    )
    key_rows = rotate(key_rows, row_pos).reshape(local_rows, HD).astype(jnp.bfloat16)
    value_rows = jnp.dot(normed, value_columns, preferred_element_type=jnp.float32).astype(
        jnp.bfloat16
    )
    key_values = jnp.concatenate([key_rows, value_rows], 1)
    window_first = window_starts(window_lengths, row_pos)
    caption_rows = is_caption == 1
    row_block = jnp.arange(local_rows, dtype=jnp.int32) // BLOCK
    span_end = span_blocks[:, 1][row_block]
    all_spans = lax.all_gather(span_blocks, "seq", axis=0, tiled=True)
    pieces = key_values.reshape(blocks_dev, ranks, BLOCK // ranks, 2 * HD)
    layout = lax.all_to_all(pieces, "seq", split_axis=1, concat_axis=1, tiled=True)
    offsets = jnp.arange(span_most, dtype=jnp.int32)
    span_wanted = all_spans[:, 0].reshape(ranks, blocks_dev, 1) + offsets[None, None, :]
    span_wanted = span_wanted.reshape(ranks, blocks_dev * span_most).T
    own_starts = span_blocks[:, 0]
    span_pos = (
        (own_starts[:, None] + offsets[None, :])[:, :, None] * BLOCK
        + jnp.arange(BLOCK, dtype=jnp.int32)[None, None, :]
    ).reshape(-1)
    span_owner = jnp.arange(blocks_dev * span_most * BLOCK, dtype=jnp.int32) // (span_most * BLOCK)
    span_ok = (span_owner[None, :] == row_block[:, None]) & (
        span_pos[None, :] // BLOCK <= span_end[:, None]
    )
    span_ok = span_ok & caption_rows[:, None] & ~inside(window_first, row_pos, span_pos)
    start_state = (
        jnp.full((local_rows, head_dev), lowest_start, jnp.float32),
        jnp.zeros((local_rows, head_dev), jnp.float32),
        jnp.zeros((local_rows, head_dev, HD), jnp.float32),
    )
    near_index = jnp.arange(window_back + blocks_dev, dtype=jnp.int32)
    near_wanted = (
        (jnp.arange(ranks, dtype=jnp.int32) * blocks_dev)[None, :]
        - window_back
        + near_index[:, None]
    )
    wanted = jnp.concatenate([near_wanted, span_wanted], 0)
    delivered = lax.all_to_all(
        select(layout, wanted, total_blocks), "seq", split_axis=1, concat_axis=1, tiled=True
    )
    gathered = delivered.reshape(-1, 2 * HD)
    near_pos = (first_pos // BLOCK - window_back) * BLOCK + jnp.arange(
        (window_back + blocks_dev) * BLOCK, dtype=jnp.int32
    )
    allowed = jnp.concatenate([inside(window_first, row_pos, near_pos), span_ok], 1)
    softmax_state = absorb_sliced(start_state, queries, gathered, allowed)
    _, denominator, weighted = softmax_state
    return (
        (weighted / denominator[..., None]).reshape(local_rows, head_dev * HD).astype(jnp.bfloat16)
    )


def vmem(count):
    return [pl.BlockSpec(memory_space=pltpu.VMEM)] * count


def smem(count):
    return [pl.BlockSpec(memory_space=pltpu.SMEM)] * count


def grant(mebibytes):
    return pltpu.CompilerParams(vmem_limit_bytes=mebibytes << 20)


def near_core(array):
    return pltpu.with_memory_space_constraint(array, pltpu.VMEM)


def turn(u, cosine, sine):
    return u * cosine + pltpu.roll(u, u.shape[-1] // 2, 1) * sine


def tables(cosine, sine):
    c, s = cosine[...], sine[...]
    return jnp.concatenate([c, c], 1), jnp.concatenate([-s, s], 1)


def load_kernel(sharers, tokens, gain, key_weight, value_weight, query_weight, caption, *refs):
    outs, sems = refs[:-1], refs[-1]
    tokens_out, gain_out, weight_out, query_out, caption_out = outs
    column = pl.multiple_of(lax.axis_index("head") // sharers * HD, HD)
    pairs = (
        (key_weight.at[:, pl.ds(column, HD)], weight_out.at[:, :HD]),
        (value_weight.at[:, pl.ds(column, HD)], weight_out.at[:, HD:]),
        (tokens, tokens_out),
        (gain, gain_out),
        (caption, caption_out),
        (query_weight, query_out),
    )
    copies = [pltpu.make_async_copy(a, b, sems.at[i]) for i, (a, b) in enumerate(pairs)]
    for copy in copies:
        copy.start()
    for copy in copies:
        copy.wait()


def squares_kernel(*refs):
    parts, out = refs[:-1], refs[-1]
    total = None
    for part in parts:
        hidden = part[...].astype(jnp.float32)
        for begin in range(0, hidden.shape[1], out.shape[1]):
            piece = hidden[:, begin : begin + out.shape[1]]
            total = piece * piece if total is None else total + piece * piece
    out[...] = total


def kv_kernel(squares, x0, x1, x2, x3, gain, weight, cosine, sine, kv_out, normed_out):
    depth = x0.shape[1]
    parts = (x0, x1, x2, x3)
    me = lax.axis_index("head")
    hidden = x3[...].astype(jnp.float32)
    total = squares[...]
    for begin in range(0, depth, total.shape[1]):
        piece = hidden[:, begin : begin + total.shape[1]]
        total = total + piece * piece
    total = jnp.sum(total, -1, keepdims=True)
    scale = lax.rsqrt(total / (depth * len(parts)) + norm_eps)
    both = None
    for order, part in enumerate(parts):
        first = pl.multiple_of(jnp.bitwise_xor(me, order) * depth, depth)
        span = pl.ds(first, depth)
        normed = (part[...].astype(jnp.float32) * scale * gain[:, span]).astype(jnp.bfloat16)
        normed_out[:, span] = normed
        product = jnp.dot(normed, weight[span, :], preferred_element_type=jnp.float32)
        both = product if both is None else both + product
    kv_out[:, :HD] = turn(both[:, :HD], *tables(cosine, sine)).astype(jnp.bfloat16)
    kv_out[:, HD:] = both[:, HD:].astype(jnp.bfloat16)


def block_of(offset):
    odd = lax.rem(lax.axis_index("head"), 2)
    return jnp.bitwise_xor(lax.axis_index("seq"), offset[0] + odd * (offset[1] - offset[0]))


def fold(q, bias, columns, kv, scores, rounded, old, new):
    rows = bias.shape[0]
    scores[...] = lax.dot_general(
        q[...],
        jnp.concatenate([block[:, :HD] for block in kv], 0),
        (((1,), (1,)), ((), ())),
        preferred_element_type=jnp.float32,
    )
    width = len(kv) * BLOCK
    highs, totals = [], []
    for begin in range(0, q.shape[0], rows):
        part = slice(begin, begin + rows)
        s = scores[part, :width] + jnp.concatenate([bias[:, c : c + BLOCK] for c in columns], 1)
        highest = jnp.broadcast_to(jnp.max(s, -1, keepdims=True), (rows, BLOCK))
        if old is not None:
            highest = jnp.maximum(highest, old[0][part, :])
        total = None
        for i in range(len(kv)):
            piece = slice(i * BLOCK, (i + 1) * BLOCK)
            weights = jnp.exp(s[:, piece] - highest)
            rounded[part, piece] = weights.astype(jnp.bfloat16)
            total = weights if total is None else total + weights
        highs.append(highest)
        totals.append(total)
    stacked = jnp.concatenate([block[:, HD:] for block in kv], 0)
    mixed = jnp.dot(rounded[:, :width], stacked, preferred_element_type=jnp.float32)
    for head, (highest, total) in enumerate(zip(highs, totals)):
        part = slice(head * rows, (head + 1) * rows)
        out = mixed[part, :]
        if old is not None:
            rescale = jnp.exp(old[0][part, :] - highest)
            total = total + rescale * old[1][part, :]
            out = out + rescale * old[2][part, :]
        new(head, part, highest, total, out)


def keep(state):
    def new(_, part, *values):
        for ref, value in zip(state, values):
            ref[part, :] = value

    return new


def query_kernel(
    offsets, lengths, spans, normed, weight, cosine, sine, caption, own, *refs
):
    (q, bias), state, (scores, rounded) = refs[:2], refs[2:5], refs[5:]
    rows = normed.shape[0]
    rank = lax.axis_index("seq")
    product = jnp.dot(normed[...], weight[...], preferred_element_type=jnp.float32)
    c, s = tables(cosine, sine)
    for begin in range(0, product.shape[1], HD):
        turned = turn(product[:, begin : begin + HD], c, s)
        first = begin // HD * rows
        q[first : first + rows, :] = (turned * HD ** (-0.5)).astype(jnp.bfloat16)
    row_pos = rank * rows + lax.broadcasted_iota(jnp.int32, (rows, BLOCK), 0)
    first_row = jnp.zeros((rows, BLOCK), jnp.int32)
    begin = jnp.int32(0)
    for w in range(lengths.shape[0]):
        end = begin + lengths[w]
        within = (row_pos >= begin) & (row_pos < end)
        first_row = jnp.where(within, begin, first_row)
        begin = end
    is_caption = jnp.broadcast_to(caption[...], (rows, rows)).T == 1
    for order, offset in enumerate(offsets):
        block = block_of(offset)
        key_pos = block * BLOCK + lax.broadcasted_iota(jnp.int32, (rows, BLOCK), 1)
        near = (first_row <= key_pos) & (key_pos <= row_pos)
        reached = (spans[0, 0] <= block) & (block <= spans[0, 1])
        allowed = near | (is_caption & reached)
        bias[:, order * BLOCK : (order + 1) * BLOCK] = jnp.where(allowed, 0.0, -jnp.inf)
    fold(q, bias, [0], [own], scores, rounded, None, keep(state))


def middle_kernel(columns, q, bias, *refs):
    old, kv = refs[:3], refs[3 : 3 + len(columns)]
    state, (scores, rounded) = refs[3 + len(columns) : 6 + len(columns)], refs[6 + len(columns) :]
    fold(q, bias, columns, kv, scores, rounded, old, keep(state))


def last_kernel(columns, q, bias, *refs):
    old, kv = refs[:3], refs[3 : 3 + len(columns)]
    out, scores, rounded = refs[3 + len(columns) :]

    def new(head, _, highest, total, mixed):
        denominator = jnp.sum(total, -1, keepdims=True)
        out[:, head * HD : (head + 1) * HD] = (mixed / denominator).astype(jnp.bfloat16)

    fold(q, bias, columns, kv, scores, rounded, old, new)


def everywhere(
    tokens,
    norm_gain,
    query_weight,
    key_weight,
    value_weight,
    window_lengths,
    is_caption,
    span_blocks,
):
    ranks, groups = lax.axis_size("seq"), lax.axis_size("head")
    rank = lax.axis_index("seq")
    rows = tokens.shape[0]
    head_dev = query_weight.shape[1] // HD

    def move(array, shift):
        pairs = [
            (r * groups + g, (r ^ shift(g)[0]) * groups + (g ^ shift(g)[1]))
            for r in range(ranks)
            for g in range(groups)
        ]
        return lax.ppermute(array, ("seq", "head"), pairs)

    across = move(tokens, lambda g: (0, 2))
    beside = move(tokens, lambda g: (0, 1))
    features = query_weight.shape[0]
    token_copy, gain, kv_weight, wide, captions = pl.pallas_call(
        functools.partial(load_kernel, H // KV // head_dev),
        out_shape=(
            pltpu.VMEM(tokens.shape, tokens.dtype),
            pltpu.VMEM((1, features), norm_gain.dtype),
            pltpu.VMEM((features, 2 * HD), key_weight.dtype),
            pltpu.VMEM(query_weight.shape, query_weight.dtype),
            pltpu.VMEM((1, rows), is_caption.dtype),
        ),
        in_specs=[pl.BlockSpec(memory_space=pltpu.HBM)] * 6,
        out_specs=tuple(vmem(5)),
        scratch_shapes=[pltpu.SemaphoreType.DMA((6,))],
        compiler_params=grant(2),
        name="load",
    )(
        *[
            pltpu.with_memory_space_constraint(array, pltpu.HBM)
            for array in (
                tokens,
                norm_gain[None, :],
                key_weight,
                value_weight,
                query_weight,
                is_caption[None, :],
            )
        ]
    )
    half = HD // 2
    frequency = rope_base ** (-jnp.arange(half, dtype=jnp.float32) * 2.0 / HD)
    row_pos = rank * rows + jnp.arange(rows, dtype=jnp.int32)
    angles = row_pos.astype(jnp.float32)[:, None] * frequency[None, :]
    cosine, sine = near_core(jnp.cos(angles)), near_core(jnp.sin(angles))
    fourth = move(across, lambda g: (0, 1))

    squares = pl.pallas_call(
        squares_kernel,
        out_shape=pltpu.VMEM((rows, HD), jnp.float32),
        in_specs=vmem(3),
        out_specs=vmem(1)[0],
        compiler_params=grant(2),
        name="squares",
    )(near_core(token_copy), near_core(beside), near_core(across))
    key_values, normed = pl.pallas_call(
        kv_kernel,
        out_shape=(
            pltpu.VMEM((rows, 2 * HD), jnp.bfloat16),
            pltpu.VMEM((rows, features), jnp.bfloat16),
        ),
        in_specs=vmem(9),
        out_specs=tuple(vmem(2)),
        compiler_params=grant(6),
        name="keys_values",
    )(
        near_core(squares),
        near_core(token_copy),
        near_core(beside),
        near_core(across),
        near_core(fourth),
        near_core(gain),
        near_core(kv_weight),
        cosine,
        sine,
    )

    far = ranks // 2
    tall = rows * head_dev

    def swapped(array):
        return move(array, lambda g: (0, 1))

    def split(array, both):
        return move(array, lambda g: (both[g % 2], 0))

    column = split(key_values, (far, far | 2))
    row = split(key_values, (2, 1))
    corner = split(key_values, (3, 3))
    diagonal = split(key_values, (far | 1, far | 3))
    held = [
        ((0, 0), key_values),
        ((2, 1), row),
        ((1, 2), swapped(row)),
        ((far, far | 2), column),
        ((far | 2, far), swapped(column)),
        ((far | 1, far | 3), diagonal),
        ((3, 3), corner),
        ((far | 3, far | 1), swapped(diagonal)),
    ]
    offsets, arrays = [offset for offset, _ in held], [near_core(array) for _, array in held]
    state = [pltpu.VMEM((tall, BLOCK), jnp.float32)] * 2 + [pltpu.VMEM((tall, HD), jnp.float32)]

    def work(count):
        return [
            pltpu.VMEM((tall, count * BLOCK), jnp.float32),
            pltpu.VMEM((tall, count * BLOCK), jnp.bfloat16),
        ]

    q, bias, *partial = pl.pallas_call(
        functools.partial(query_kernel, offsets),
        out_shape=(
            pltpu.VMEM((tall, HD), jnp.bfloat16),
            pltpu.VMEM((rows, ranks * BLOCK), jnp.float32),
            *state,
        ),
        in_specs=smem(2) + vmem(6),
        out_specs=tuple(vmem(5)),
        scratch_shapes=work(1),
        compiler_params=grant(6),
        name="queries",
    )(
        window_lengths,
        span_blocks,
        near_core(normed),
        near_core(wide),
        cosine,
        sine,
        near_core(captions),
        arrays[0],
    )

    def columns(first, end):
        return [order * BLOCK for order in range(first, end)]

    later = ranks - 2
    partial = pl.pallas_call(
        functools.partial(middle_kernel, columns(1, later)),
        out_shape=tuple(state),
        in_specs=vmem(5 + later - 1),
        out_specs=tuple(vmem(3)),
        scratch_shapes=work(later - 1),
        compiler_params=grant(6),
        name="middle",
    )(*[near_core(array) for array in (q, bias, *partial)], *arrays[1:later])
    return pl.pallas_call(
        functools.partial(last_kernel, columns(later, ranks)),
        out_shape=jax.ShapeDtypeStruct((rows, head_dev * HD), jnp.bfloat16),
        in_specs=vmem(5 + ranks - later),
        out_specs=vmem(1)[0],
        scratch_shapes=work(ranks - later),
        compiler_params=grant(6),
        name="last",
    )(*[near_core(array) for array in (q, bias, *partial)], *arrays[later:])


near_plan = (0, 1, 2, 3)
feature_plan = (0, 1, 2, 3)


def gathers_all(mesh, rows, head_dev):
    ranks, groups = mesh.shape["seq"], mesh.shape["head"]
    total_blocks = ranks * rows // BLOCK
    window = min(window_cap, total_blocks * BLOCK // 4)
    read = (window + BLOCK - 2) // BLOCK + 1 + min(span_cap, total_blocks // 4)
    shared = groups % 2 == 0 and (H // KV) % (2 * head_dev) == 0
    fits = rows == BLOCK and ranks == 2 * len(near_plan) and groups == len(feature_plan)
    return shared and fits and 2 * read >= total_blocks


def solution(mesh):
    in_specs = (P("seq", "head"), P(), P(None, "head"), P(), P(), P(), P("seq"), P("seq", None))
    out_specs = P("seq", "head")

    def per_device(*arguments):
        rows, head_dev = arguments[0].shape[0], arguments[2].shape[1] // HD
        if not gathers_all(mesh, rows, head_dev):
            return by_request(*arguments)
        return everywhere(*arguments)

    return jax.shard_map(
        per_device, mesh=mesh, in_specs=in_specs, out_specs=out_specs, check_vma=False
    )
```

```python
import functools

import jax
import jax.numpy as jnp
from jax import lax
from jax.experimental import pallas as pl
from jax.experimental.pallas import tpu as pltpu
from jax.sharding import PartitionSpec as P

H = 16
KV = 2
HD = 128
BLOCK = 128


norm_eps = 1e-05
rope_base = 500000.0
window_cap = 4096
span_cap = 8
slice_blocks = 8
lowest_start = -1e30


def rotate(vectors, position):
    half_size = vectors.shape[-1] // 2
    frequency = rope_base ** (-jnp.arange(half_size, dtype=jnp.float32) * 2.0 / vectors.shape[-1])
    angles = position.astype(jnp.float32)[:, None] * frequency[None, :]
    cosine = jnp.cos(angles)[:, None, :]
    sine_part = jnp.sin(angles)[:, None, :]
    first_half = vectors[..., :half_size]
    second_half = vectors[..., half_size:]
    return jnp.concatenate(
        [
            first_half * cosine - second_half * sine_part,
            second_half * cosine + first_half * sine_part,
        ],
        -1,
    )


def rms_normed(tokens, norm_gain):
    hidden = tokens.astype(jnp.float32)
    scale = lax.rsqrt(jnp.mean(hidden * hidden, -1, keepdims=True) + norm_eps)
    return (hidden * scale * norm_gain[None, :]).astype(jnp.bfloat16)


def window_starts(window_lengths, position):
    window_ends = jnp.cumsum(window_lengths)
    begins = window_ends - window_lengths
    within = (begins[None, :] <= position[:, None]) & (position[:, None] < window_ends[None, :])
    return jnp.sum(jnp.where(within, begins[None, :], 0), 1)


def inside(first_row, row_pos, key_pos):
    return (first_row[:, None] <= key_pos[None, :]) & (key_pos[None, :] <= row_pos[:, None])


def absorb(softmax_state, queries, key_values, allowed):
    highest, denominator, weighted = softmax_state
    head_size = queries.shape[-1]
    scores = jnp.einsum(
        "rhd,nd->rhn", queries, key_values[:, :head_size], preferred_element_type=jnp.float32
    )
    scores = jnp.where(allowed[:, None, :], scores, -jnp.inf)
    updated = jnp.maximum(highest, jnp.max(scores, -1))
    rescale = jnp.exp(highest - updated)
    weights = jnp.exp(scores - updated[..., None])
    denominator = rescale * denominator + jnp.sum(weights, -1)
    weighted = rescale[..., None] * weighted + jnp.einsum(
        "rhn,nd->rhd",
        weights.astype(jnp.bfloat16),
        key_values[:, head_size:],
        preferred_element_type=jnp.float32,
    )
    return (updated, denominator, weighted)


def absorb_sliced(softmax_state, queries, key_values, allowed):
    key_count = key_values.shape[0]
    piece = slice_blocks * BLOCK
    for begin in range(0, key_count, piece):
        finish = min(begin + piece, key_count)
        softmax_state = absorb(
            softmax_state, queries, key_values[begin:finish], allowed[:, begin:finish]
        )
    return softmax_state


def select(layout, wanted, total_blocks):
    blocks_dev = layout.shape[0]
    clipped = jnp.clip(wanted, 0, total_blocks - 1)
    return layout[clipped % blocks_dev, clipped // blocks_dev]


def by_request(
    tokens,
    norm_gain,
    query_weight,
    key_weight,
    value_weight,
    window_lengths,
    is_caption,
    span_blocks,
):
    ranks = lax.axis_size("seq")
    device_rank = lax.axis_index("seq")
    features = lax.all_gather(tokens, "head", axis=1, tiled=True)
    local_rows = features.shape[0]
    blocks_dev = local_rows // BLOCK
    total_blocks = blocks_dev * ranks
    window = min(window_cap, total_blocks * BLOCK // 4)
    span_most = min(span_cap, total_blocks // 4)
    window_back = (window + BLOCK - 2) // BLOCK
    first_pos = device_rank * local_rows
    row_pos = first_pos + jnp.arange(local_rows, dtype=jnp.int32)
    normed = rms_normed(features, norm_gain)
    head_dev = query_weight.shape[1] // HD
    kv_index = lax.axis_index("head") * head_dev // (H // KV)
    queries = jnp.dot(normed, query_weight, preferred_element_type=jnp.float32).reshape(
        local_rows, head_dev, HD
    )
    queries = (rotate(queries, row_pos) * HD ** (-0.5)).astype(jnp.bfloat16)
    key_columns = lax.dynamic_slice_in_dim(key_weight, kv_index * HD, HD, 1)
    value_columns = lax.dynamic_slice_in_dim(value_weight, kv_index * HD, HD, 1)
    key_rows = jnp.dot(normed, key_columns, preferred_element_type=jnp.float32).reshape(
        local_rows, 1, HD
    )
    key_rows = rotate(key_rows, row_pos).reshape(local_rows, HD).astype(jnp.bfloat16)
    value_rows = jnp.dot(normed, value_columns, preferred_element_type=jnp.float32).astype(
        jnp.bfloat16
    )
    key_values = jnp.concatenate([key_rows, value_rows], 1)
    window_first = window_starts(window_lengths, row_pos)
    caption_rows = is_caption == 1
    row_block = jnp.arange(local_rows, dtype=jnp.int32) // BLOCK
    span_end = span_blocks[:, 1][row_block]
    all_spans = lax.all_gather(span_blocks, "seq", axis=0, tiled=True)
    pieces = key_values.reshape(blocks_dev, ranks, BLOCK // ranks, 2 * HD)
    layout = lax.all_to_all(pieces, "seq", split_axis=1, concat_axis=1, tiled=True)
    offsets = jnp.arange(span_most, dtype=jnp.int32)
    span_wanted = all_spans[:, 0].reshape(ranks, blocks_dev, 1) + offsets[None, None, :]
    span_wanted = span_wanted.reshape(ranks, blocks_dev * span_most).T
    own_starts = span_blocks[:, 0]
    span_pos = (
        (own_starts[:, None] + offsets[None, :])[:, :, None] * BLOCK
        + jnp.arange(BLOCK, dtype=jnp.int32)[None, None, :]
    ).reshape(-1)
    span_owner = jnp.arange(blocks_dev * span_most * BLOCK, dtype=jnp.int32) // (span_most * BLOCK)
    span_ok = (span_owner[None, :] == row_block[:, None]) & (
        span_pos[None, :] // BLOCK <= span_end[:, None]
    )
    span_ok = span_ok & caption_rows[:, None] & ~inside(window_first, row_pos, span_pos)
    start_state = (
        jnp.full((local_rows, head_dev), lowest_start, jnp.float32),
        jnp.zeros((local_rows, head_dev), jnp.float32),
        jnp.zeros((local_rows, head_dev, HD), jnp.float32),
    )
    near_index = jnp.arange(window_back + blocks_dev, dtype=jnp.int32)
    near_wanted = (
        (jnp.arange(ranks, dtype=jnp.int32) * blocks_dev)[None, :]
        - window_back
        + near_index[:, None]
    )
    wanted = jnp.concatenate([near_wanted, span_wanted], 0)
    delivered = lax.all_to_all(
        select(layout, wanted, total_blocks), "seq", split_axis=1, concat_axis=1, tiled=True
    )
    gathered = delivered.reshape(-1, 2 * HD)
    near_pos = (first_pos // BLOCK - window_back) * BLOCK + jnp.arange(
        (window_back + blocks_dev) * BLOCK, dtype=jnp.int32
    )
    allowed = jnp.concatenate([inside(window_first, row_pos, near_pos), span_ok], 1)
    softmax_state = absorb_sliced(start_state, queries, gathered, allowed)
    _, denominator, weighted = softmax_state
    return (
        (weighted / denominator[..., None]).reshape(local_rows, head_dev * HD).astype(jnp.bfloat16)
    )


def vmem(count):
    return [pl.BlockSpec(memory_space=pltpu.VMEM)] * count


def smem(count):
    return [pl.BlockSpec(memory_space=pltpu.SMEM)] * count


def grant(mebibytes):
    return pltpu.CompilerParams(vmem_limit_bytes=mebibytes << 20)


def near_core(array):
    return pltpu.with_memory_space_constraint(array, pltpu.VMEM)


def turn(u, cosine, sine):
    return u * cosine + pltpu.roll(u, u.shape[-1] // 2, 1) * sine


def tables(cosine, sine):
    c, s = cosine[...], sine[...]
    return jnp.concatenate([c, c], 1), jnp.concatenate([-s, s], 1)


def load_kernel(sharers, tokens, gain, key_weight, value_weight, query_weight, caption, *refs):
    outs, sems = refs[:-1], refs[-1]
    tokens_out, gain_out, weight_out, query_out, caption_out = outs
    column = pl.multiple_of(lax.axis_index("head") // sharers * HD, HD)
    pairs = (
        (key_weight.at[:, pl.ds(column, HD)], weight_out.at[:, :HD]),
        (value_weight.at[:, pl.ds(column, HD)], weight_out.at[:, HD:]),
        (tokens, tokens_out),
        (gain, gain_out),
        (caption, caption_out),
        (query_weight, query_out),
    )
    copies = [pltpu.make_async_copy(a, b, sems.at[i]) for i, (a, b) in enumerate(pairs)]
    for copy in copies:
        copy.start()
    for copy in copies:
        copy.wait()


def squares_kernel(*refs):
    parts, out = refs[:-1], refs[-1]
    total = None
    for part in parts:
        hidden = part[...].astype(jnp.float32)
        for begin in range(0, hidden.shape[1], out.shape[1]):
            piece = hidden[:, begin : begin + out.shape[1]]
            total = piece * piece if total is None else total + piece * piece
    out[...] = total


def kv_kernel(squares, x0, x1, x2, x3, gain, weight, cosine, sine, kv_out, normed_out):
    depth = x0.shape[1]
    parts = (x0, x1, x2, x3)
    me = lax.axis_index("head")
    hidden = x3[...].astype(jnp.float32)
    total = squares[...]
    for begin in range(0, depth, total.shape[1]):
        piece = hidden[:, begin : begin + total.shape[1]]
        total = total + piece * piece
    total = jnp.sum(total, -1, keepdims=True)
    scale = lax.rsqrt(total / (depth * len(parts)) + norm_eps)
    both = None
    for order, part in enumerate(parts):
        first = pl.multiple_of(jnp.bitwise_xor(me, order) * depth, depth)
        span = pl.ds(first, depth)
        normed = (part[...].astype(jnp.float32) * scale * gain[:, span]).astype(jnp.bfloat16)
        normed_out[:, span] = normed
        product = jnp.dot(normed, weight[span, :], preferred_element_type=jnp.float32)
        both = product if both is None else both + product
    kv_out[:, :HD] = turn(both[:, :HD], *tables(cosine, sine)).astype(jnp.bfloat16)
    kv_out[:, HD:] = both[:, HD:].astype(jnp.bfloat16)


def block_of(offset):
    odd = lax.rem(lax.axis_index("head"), 2)
    return jnp.bitwise_xor(lax.axis_index("seq"), offset[0] + odd * (offset[1] - offset[0]))


def fold(q, bias, columns, kv, scores, rounded, old, new):
    rows = bias.shape[0]
    scores[...] = lax.dot_general(
        q[...],
        jnp.concatenate([block[:, :HD] for block in kv], 0),
        (((1,), (1,)), ((), ())),
        preferred_element_type=jnp.float32,
    )
    width = len(kv) * BLOCK
    highs, totals = [], []
    for begin in range(0, q.shape[0], rows):
        part = slice(begin, begin + rows)
        s = scores[part, :width] + jnp.concatenate([bias[:, c : c + BLOCK] for c in columns], 1)
        highest = jnp.broadcast_to(jnp.max(s, -1, keepdims=True), (rows, BLOCK))
        if old is not None:
            highest = jnp.maximum(highest, old[0][part, :])
        total = None
        for i in range(len(kv)):
            piece = slice(i * BLOCK, (i + 1) * BLOCK)
            weights = jnp.exp(s[:, piece] - highest)
            rounded[part, piece] = weights.astype(jnp.bfloat16)
            total = weights if total is None else total + weights
        highs.append(highest)
        totals.append(total)
    stacked = jnp.concatenate([block[:, HD:] for block in kv], 0)
    mixed = jnp.dot(rounded[:, :width], stacked, preferred_element_type=jnp.float32)
    for head, (highest, total) in enumerate(zip(highs, totals)):
        part = slice(head * rows, (head + 1) * rows)
        out = mixed[part, :]
        if old is not None:
            rescale = jnp.exp(old[0][part, :] - highest)
            total = total + rescale * old[1][part, :]
            out = out + rescale * old[2][part, :]
        new(head, part, highest, total, out)


def keep(state):
    def new(_, part, *values):
        for ref, value in zip(state, values):
            ref[part, :] = value

    return new


def query_kernel(
    offsets, lengths, spans, normed, weight, cosine, sine, caption, own, *refs
):
    (q, bias), state, (scores, rounded) = refs[:2], refs[2:5], refs[5:]
    rows = normed.shape[0]
    rank = lax.axis_index("seq")
    product = jnp.dot(normed[...], weight[...], preferred_element_type=jnp.float32)
    c, s = tables(cosine, sine)
    for begin in range(0, product.shape[1], HD):
        turned = turn(product[:, begin : begin + HD], c, s)
        first = begin // HD * rows
        q[first : first + rows, :] = (turned * HD ** (-0.5)).astype(jnp.bfloat16)
    row_pos = rank * rows + lax.broadcasted_iota(jnp.int32, (rows, BLOCK), 0)
    first_row = jnp.zeros((rows, BLOCK), jnp.int32)
    begin = jnp.int32(0)
    for w in range(lengths.shape[0]):
        end = begin + lengths[w]
        within = (row_pos >= begin) & (row_pos < end)
        first_row = jnp.where(within, begin, first_row)
        begin = end
    is_caption = jnp.broadcast_to(caption[...], (rows, rows)).T == 1
    for order, offset in enumerate(offsets):
        block = block_of(offset)
        key_pos = block * BLOCK + lax.broadcasted_iota(jnp.int32, (rows, BLOCK), 1)
        near = (first_row <= key_pos) & (key_pos <= row_pos)
        reached = (spans[0, 0] <= block) & (block <= spans[0, 1])
        allowed = near | (is_caption & reached)
        bias[:, order * BLOCK : (order + 1) * BLOCK] = jnp.where(allowed, 0.0, -jnp.inf)
    fold(q, bias, [0], [own], scores, rounded, None, keep(state))


def middle_kernel(columns, q, bias, *refs):
    old, kv = refs[:3], refs[3 : 3 + len(columns)]
    state, (scores, rounded) = refs[3 + len(columns) : 6 + len(columns)], refs[6 + len(columns) :]
    fold(q, bias, columns, kv, scores, rounded, old, keep(state))


def last_kernel(columns, q, bias, *refs):
    old, kv = refs[:3], refs[3 : 3 + len(columns)]
    out, scores, rounded = refs[3 + len(columns) :]

    def new(head, _, highest, total, mixed):
        denominator = jnp.sum(total, -1, keepdims=True)
        out[:, head * HD : (head + 1) * HD] = (mixed / denominator).astype(jnp.bfloat16)

    fold(q, bias, columns, kv, scores, rounded, old, new)


def everywhere(
    tokens,
    norm_gain,
    query_weight,
    key_weight,
    value_weight,
    window_lengths,
    is_caption,
    span_blocks,
):
    ranks, groups = lax.axis_size("seq"), lax.axis_size("head")
    rank = lax.axis_index("seq")
    rows = tokens.shape[0]
    head_dev = query_weight.shape[1] // HD

    def move(array, shift):
        pairs = [
            (r * groups + g, (r ^ shift(g)[0]) * groups + (g ^ shift(g)[1]))
            for r in range(ranks)
            for g in range(groups)
        ]
        return lax.ppermute(array, ("seq", "head"), pairs)

    across = move(tokens, lambda g: (0, 2))
    beside = move(tokens, lambda g: (0, 1))
    features = query_weight.shape[0]
    token_copy, gain, kv_weight, wide, captions = pl.pallas_call(
        functools.partial(load_kernel, H // KV // head_dev),
        out_shape=(
            pltpu.VMEM(tokens.shape, tokens.dtype),
            pltpu.VMEM((1, features), norm_gain.dtype),
            pltpu.VMEM((features, 2 * HD), key_weight.dtype),
            pltpu.VMEM(query_weight.shape, query_weight.dtype),
            pltpu.VMEM((1, rows), is_caption.dtype),
        ),
        in_specs=[pl.BlockSpec(memory_space=pltpu.HBM)] * 6,
        out_specs=tuple(vmem(5)),
        scratch_shapes=[pltpu.SemaphoreType.DMA((6,))],
        compiler_params=grant(2),
        name="load",
    )(
        *[
            pltpu.with_memory_space_constraint(array, pltpu.HBM)
            for array in (
                tokens,
                norm_gain[None, :],
                key_weight,
                value_weight,
                query_weight,
                is_caption[None, :],
            )
        ]
    )
    half = HD // 2
    frequency = rope_base ** (-jnp.arange(half, dtype=jnp.float32) * 2.0 / HD)
    row_pos = rank * rows + jnp.arange(rows, dtype=jnp.int32)
    angles = row_pos.astype(jnp.float32)[:, None] * frequency[None, :]
    cosine, sine = near_core(jnp.cos(angles)), near_core(jnp.sin(angles))
    fourth = move(across, lambda g: (0, 1))

    squares = pl.pallas_call(
        squares_kernel,
        out_shape=pltpu.VMEM((rows, HD), jnp.float32),
        in_specs=vmem(3),
        out_specs=vmem(1)[0],
        compiler_params=grant(2),
        name="squares",
    )(near_core(token_copy), near_core(beside), near_core(across))
    key_values, normed = pl.pallas_call(
        kv_kernel,
        out_shape=(
            pltpu.VMEM((rows, 2 * HD), jnp.bfloat16),
            pltpu.VMEM((rows, features), jnp.bfloat16),
        ),
        in_specs=vmem(9),
        out_specs=tuple(vmem(2)),
        compiler_params=grant(6),
        name="keys_values",
    )(
        near_core(squares),
        near_core(token_copy),
        near_core(beside),
        near_core(across),
        near_core(fourth),
        near_core(gain),
        near_core(kv_weight),
        cosine,
        sine,
    )

    far = ranks // 2
    tall = rows * head_dev

    def swapped(array):
        return move(array, lambda g: (0, 1))

    def split(array, both):
        return move(array, lambda g: (both[g % 2], 0))

    column = split(key_values, (far, 2))
    diagonal = split(key_values, (far | 2, far | 1))
    row = split(key_values, (1, far | 3))
    corner = split(key_values, (3, 3))
    held = [
        ((0, 0), key_values),
        ((far, 2), column),
        ((2, far), swapped(column)),
        ((far | 2, far | 1), diagonal),
        ((far | 1, far | 2), swapped(diagonal)),
        ((1, far | 3), row),
        ((3, 3), corner),
        ((far | 3, 1), swapped(row)),
    ]
    offsets, arrays = [offset for offset, _ in held], [near_core(array) for _, array in held]
    state = [pltpu.VMEM((tall, BLOCK), jnp.float32)] * 2 + [pltpu.VMEM((tall, HD), jnp.float32)]

    def work(count):
        return [
            pltpu.VMEM((tall, count * BLOCK), jnp.float32),
            pltpu.VMEM((tall, count * BLOCK), jnp.bfloat16),
        ]

    q, bias, *partial = pl.pallas_call(
        functools.partial(query_kernel, offsets),
        out_shape=(
            pltpu.VMEM((tall, HD), jnp.bfloat16),
            pltpu.VMEM((rows, ranks * BLOCK), jnp.float32),
            *state,
        ),
        in_specs=smem(2) + vmem(6),
        out_specs=tuple(vmem(5)),
        scratch_shapes=work(1),
        compiler_params=grant(6),
        name="queries",
    )(
        window_lengths,
        span_blocks,
        near_core(normed),
        near_core(wide),
        cosine,
        sine,
        near_core(captions),
        arrays[0],
    )

    def columns(first, end):
        return [order * BLOCK for order in range(first, end)]

    early, later = ranks // 2, ranks - 2
    for first, end in ((1, early), (early, later)):
        partial = pl.pallas_call(
            functools.partial(middle_kernel, columns(first, end)),
            out_shape=tuple(state),
            in_specs=vmem(5 + end - first),
            out_specs=tuple(vmem(3)),
            scratch_shapes=work(end - first),
            compiler_params=grant(6),
        )(*[near_core(array) for array in (q, bias, *partial)], *arrays[first:end])
    return pl.pallas_call(
        functools.partial(last_kernel, columns(later, ranks)),
        out_shape=jax.ShapeDtypeStruct((rows, head_dev * HD), jnp.bfloat16),
        in_specs=vmem(5 + ranks - later),
        out_specs=vmem(1)[0],
        scratch_shapes=work(ranks - later),
        compiler_params=grant(6),
        name="last",
    )(*[near_core(array) for array in (q, bias, *partial)], *arrays[later:])


near_plan = (0, 1, 2, 3)
feature_plan = (0, 1, 2, 3)


def gathers_all(mesh, rows, head_dev):
    ranks, groups = mesh.shape["seq"], mesh.shape["head"]
    total_blocks = ranks * rows // BLOCK
    window = min(window_cap, total_blocks * BLOCK // 4)
    read = (window + BLOCK - 2) // BLOCK + 1 + min(span_cap, total_blocks // 4)
    shared = groups % 2 == 0 and (H // KV) % (2 * head_dev) == 0
    fits = rows == BLOCK and ranks == 2 * len(near_plan) and groups == len(feature_plan)
    return shared and fits and 2 * read >= total_blocks


def solution(mesh):
    in_specs = (P("seq", "head"), P(), P(None, "head"), P(), P(), P(), P("seq"), P("seq", None))
    out_specs = P("seq", "head")

    def per_device(*arguments):
        rows, head_dev = arguments[0].shape[0], arguments[2].shape[1] // HD
        if not gathers_all(mesh, rows, head_dev):
            return by_request(*arguments)
        return everywhere(*arguments)

    return jax.shard_map(
        per_device, mesh=mesh, in_specs=in_specs, out_specs=out_specs, check_vma=False
    )
```

```python
import functools

import jax
import jax.numpy as jnp
from jax import lax
from jax.experimental import pallas as pl
from jax.experimental.pallas import tpu as pltpu
from jax.sharding import PartitionSpec as P

H = 16
KV = 2
HD = 128
BLOCK = 128


norm_eps = 1e-05
rope_base = 500000.0
window_cap = 4096
span_cap = 8
slice_blocks = 8
lowest_start = -1e30


def rotate(vectors, position):
    half_size = vectors.shape[-1] // 2
    frequency = rope_base ** (-jnp.arange(half_size, dtype=jnp.float32) * 2.0 / vectors.shape[-1])
    angles = position.astype(jnp.float32)[:, None] * frequency[None, :]
    cosine = jnp.cos(angles)[:, None, :]
    sine_part = jnp.sin(angles)[:, None, :]
    first_half = vectors[..., :half_size]
    second_half = vectors[..., half_size:]
    return jnp.concatenate(
        [
            first_half * cosine - second_half * sine_part,
            second_half * cosine + first_half * sine_part,
        ],
        -1,
    )


def rms_normed(tokens, norm_gain):
    hidden = tokens.astype(jnp.float32)
    scale = lax.rsqrt(jnp.mean(hidden * hidden, -1, keepdims=True) + norm_eps)
    return (hidden * scale * norm_gain[None, :]).astype(jnp.bfloat16)


def window_starts(window_lengths, position):
    window_ends = jnp.cumsum(window_lengths)
    begins = window_ends - window_lengths
    within = (begins[None, :] <= position[:, None]) & (position[:, None] < window_ends[None, :])
    return jnp.sum(jnp.where(within, begins[None, :], 0), 1)


def inside(first_row, row_pos, key_pos):
    return (first_row[:, None] <= key_pos[None, :]) & (key_pos[None, :] <= row_pos[:, None])


def absorb(softmax_state, queries, key_values, allowed):
    highest, denominator, weighted = softmax_state
    head_size = queries.shape[-1]
    scores = jnp.einsum(
        "rhd,nd->rhn", queries, key_values[:, :head_size], preferred_element_type=jnp.float32
    )
    scores = jnp.where(allowed[:, None, :], scores, -jnp.inf)
    updated = jnp.maximum(highest, jnp.max(scores, -1))
    rescale = jnp.exp(highest - updated)
    weights = jnp.exp(scores - updated[..., None])
    denominator = rescale * denominator + jnp.sum(weights, -1)
    weighted = rescale[..., None] * weighted + jnp.einsum(
        "rhn,nd->rhd",
        weights.astype(jnp.bfloat16),
        key_values[:, head_size:],
        preferred_element_type=jnp.float32,
    )
    return (updated, denominator, weighted)


def absorb_sliced(softmax_state, queries, key_values, allowed):
    key_count = key_values.shape[0]
    piece = slice_blocks * BLOCK
    for begin in range(0, key_count, piece):
        finish = min(begin + piece, key_count)
        softmax_state = absorb(
            softmax_state, queries, key_values[begin:finish], allowed[:, begin:finish]
        )
    return softmax_state


def select(layout, wanted, total_blocks):
    blocks_dev = layout.shape[0]
    clipped = jnp.clip(wanted, 0, total_blocks - 1)
    return layout[clipped % blocks_dev, clipped // blocks_dev]


def by_request(
    tokens,
    norm_gain,
    query_weight,
    key_weight,
    value_weight,
    window_lengths,
    is_caption,
    span_blocks,
):
    ranks = lax.axis_size("seq")
    device_rank = lax.axis_index("seq")
    features = lax.all_gather(tokens, "head", axis=1, tiled=True)
    local_rows = features.shape[0]
    blocks_dev = local_rows // BLOCK
    total_blocks = blocks_dev * ranks
    window = min(window_cap, total_blocks * BLOCK // 4)
    span_most = min(span_cap, total_blocks // 4)
    window_back = (window + BLOCK - 2) // BLOCK
    first_pos = device_rank * local_rows
    row_pos = first_pos + jnp.arange(local_rows, dtype=jnp.int32)
    normed = rms_normed(features, norm_gain)
    head_dev = query_weight.shape[1] // HD
    kv_index = lax.axis_index("head") * head_dev // (H // KV)
    queries = jnp.dot(normed, query_weight, preferred_element_type=jnp.float32).reshape(
        local_rows, head_dev, HD
    )
    queries = (rotate(queries, row_pos) * HD ** (-0.5)).astype(jnp.bfloat16)
    key_columns = lax.dynamic_slice_in_dim(key_weight, kv_index * HD, HD, 1)
    value_columns = lax.dynamic_slice_in_dim(value_weight, kv_index * HD, HD, 1)
    key_rows = jnp.dot(normed, key_columns, preferred_element_type=jnp.float32).reshape(
        local_rows, 1, HD
    )
    key_rows = rotate(key_rows, row_pos).reshape(local_rows, HD).astype(jnp.bfloat16)
    value_rows = jnp.dot(normed, value_columns, preferred_element_type=jnp.float32).astype(
        jnp.bfloat16
    )
    key_values = jnp.concatenate([key_rows, value_rows], 1)
    window_first = window_starts(window_lengths, row_pos)
    caption_rows = is_caption == 1
    row_block = jnp.arange(local_rows, dtype=jnp.int32) // BLOCK
    span_end = span_blocks[:, 1][row_block]
    all_spans = lax.all_gather(span_blocks, "seq", axis=0, tiled=True)
    pieces = key_values.reshape(blocks_dev, ranks, BLOCK // ranks, 2 * HD)
    layout = lax.all_to_all(pieces, "seq", split_axis=1, concat_axis=1, tiled=True)
    offsets = jnp.arange(span_most, dtype=jnp.int32)
    span_wanted = all_spans[:, 0].reshape(ranks, blocks_dev, 1) + offsets[None, None, :]
    span_wanted = span_wanted.reshape(ranks, blocks_dev * span_most).T
    own_starts = span_blocks[:, 0]
    span_pos = (
        (own_starts[:, None] + offsets[None, :])[:, :, None] * BLOCK
        + jnp.arange(BLOCK, dtype=jnp.int32)[None, None, :]
    ).reshape(-1)
    span_owner = jnp.arange(blocks_dev * span_most * BLOCK, dtype=jnp.int32) // (span_most * BLOCK)
    span_ok = (span_owner[None, :] == row_block[:, None]) & (
        span_pos[None, :] // BLOCK <= span_end[:, None]
    )
    span_ok = span_ok & caption_rows[:, None] & ~inside(window_first, row_pos, span_pos)
    start_state = (
        jnp.full((local_rows, head_dev), lowest_start, jnp.float32),
        jnp.zeros((local_rows, head_dev), jnp.float32),
        jnp.zeros((local_rows, head_dev, HD), jnp.float32),
    )
    near_index = jnp.arange(window_back + blocks_dev, dtype=jnp.int32)
    near_wanted = (
        (jnp.arange(ranks, dtype=jnp.int32) * blocks_dev)[None, :]
        - window_back
        + near_index[:, None]
    )
    wanted = jnp.concatenate([near_wanted, span_wanted], 0)
    delivered = lax.all_to_all(
        select(layout, wanted, total_blocks), "seq", split_axis=1, concat_axis=1, tiled=True
    )
    gathered = delivered.reshape(-1, 2 * HD)
    near_pos = (first_pos // BLOCK - window_back) * BLOCK + jnp.arange(
        (window_back + blocks_dev) * BLOCK, dtype=jnp.int32
    )
    allowed = jnp.concatenate([inside(window_first, row_pos, near_pos), span_ok], 1)
    softmax_state = absorb_sliced(start_state, queries, gathered, allowed)
    _, denominator, weighted = softmax_state
    return (
        (weighted / denominator[..., None]).reshape(local_rows, head_dev * HD).astype(jnp.bfloat16)
    )


def vmem(count):
    return [pl.BlockSpec(memory_space=pltpu.VMEM)] * count


def smem(count):
    return [pl.BlockSpec(memory_space=pltpu.SMEM)] * count


def grant(mebibytes):
    return pltpu.CompilerParams(vmem_limit_bytes=mebibytes << 20)


def near_core(array):
    return pltpu.with_memory_space_constraint(array, pltpu.VMEM)


def turn(u, cosine, sine):
    return u * cosine + pltpu.roll(u, u.shape[-1] // 2, 1) * sine


def tables(cosine, sine):
    c, s = cosine[...], sine[...]
    return jnp.concatenate([c, c], 1), jnp.concatenate([-s, s], 1)


def load_kernel(sharers, tokens, gain, key_weight, value_weight, query_weight, caption, *refs):
    outs, sems = refs[:-1], refs[-1]
    tokens_out, gain_out, weight_out, query_out, caption_out = outs
    column = pl.multiple_of(lax.axis_index("head") // sharers * HD, HD)
    pairs = (
        (key_weight.at[:, pl.ds(column, HD)], weight_out.at[:, :HD]),
        (value_weight.at[:, pl.ds(column, HD)], weight_out.at[:, HD:]),
        (tokens, tokens_out),
        (gain, gain_out),
        (caption, caption_out),
        (query_weight, query_out),
    )
    copies = [pltpu.make_async_copy(a, b, sems.at[i]) for i, (a, b) in enumerate(pairs)]
    for copy in copies:
        copy.start()
    for copy in copies:
        copy.wait()


def squares_kernel(*refs):
    parts, out = refs[:-1], refs[-1]
    total = None
    for part in parts:
        hidden = part[...].astype(jnp.float32)
        for begin in range(0, hidden.shape[1], out.shape[1]):
            piece = hidden[:, begin : begin + out.shape[1]]
            total = piece * piece if total is None else total + piece * piece
    out[...] = total


def kv_kernel(squares, x0, x1, x2, x3, gain, weight, cosine, sine, kv_out, normed_out):
    depth = x0.shape[1]
    parts = (x0, x1, x2, x3)
    me = lax.axis_index("head")
    hidden = x3[...].astype(jnp.float32)
    total = squares[...]
    for begin in range(0, depth, total.shape[1]):
        piece = hidden[:, begin : begin + total.shape[1]]
        total = total + piece * piece
    total = jnp.sum(total, -1, keepdims=True)
    scale = lax.rsqrt(total / (depth * len(parts)) + norm_eps)
    both = None
    for order, part in enumerate(parts):
        first = pl.multiple_of(jnp.bitwise_xor(me, order) * depth, depth)
        span = pl.ds(first, depth)
        normed = (part[...].astype(jnp.float32) * scale * gain[:, span]).astype(jnp.bfloat16)
        normed_out[:, span] = normed
        product = jnp.dot(normed, weight[span, :], preferred_element_type=jnp.float32)
        both = product if both is None else both + product
    kv_out[:, :HD] = turn(both[:, :HD], *tables(cosine, sine)).astype(jnp.bfloat16)
    kv_out[:, HD:] = both[:, HD:].astype(jnp.bfloat16)


def block_of(offset):
    odd = lax.rem(lax.axis_index("head"), 2)
    return jnp.bitwise_xor(lax.axis_index("seq"), offset[0] + odd * (offset[1] - offset[0]))


def fold(q, bias, columns, kv, scores, rounded, old, new):
    rows = bias.shape[0]
    scores[...] = lax.dot_general(
        q[...],
        jnp.concatenate([block[:, :HD] for block in kv], 0),
        (((1,), (1,)), ((), ())),
        preferred_element_type=jnp.float32,
    )
    width = len(kv) * BLOCK
    highs, totals = [], []
    for begin in range(0, q.shape[0], rows):
        part = slice(begin, begin + rows)
        s = scores[part, :width] + jnp.concatenate([bias[:, c : c + BLOCK] for c in columns], 1)
        highest = jnp.broadcast_to(jnp.max(s, -1, keepdims=True), (rows, BLOCK))
        if old is not None:
            highest = jnp.maximum(highest, old[0][part, :])
        total = None
        for i in range(len(kv)):
            piece = slice(i * BLOCK, (i + 1) * BLOCK)
            weights = jnp.exp(s[:, piece] - highest)
            rounded[part, piece] = weights.astype(jnp.bfloat16)
            total = weights if total is None else total + weights
        highs.append(highest)
        totals.append(total)
    stacked = jnp.concatenate([block[:, HD:] for block in kv], 0)
    mixed = jnp.dot(rounded[:, :width], stacked, preferred_element_type=jnp.float32)
    for head, (highest, total) in enumerate(zip(highs, totals)):
        part = slice(head * rows, (head + 1) * rows)
        out = mixed[part, :]
        if old is not None:
            rescale = jnp.exp(old[0][part, :] - highest)
            total = total + rescale * old[1][part, :]
            out = out + rescale * old[2][part, :]
        new(head, part, highest, total, out)


def keep(state):
    def new(_, part, *values):
        for ref, value in zip(state, values):
            ref[part, :] = value

    return new


def query_kernel(
    offsets, lengths, spans, normed, weight, cosine, sine, caption, own, *refs
):
    (q, bias), state, (scores, rounded) = refs[:2], refs[2:5], refs[5:]
    rows = normed.shape[0]
    rank = lax.axis_index("seq")
    product = jnp.dot(normed[...], weight[...], preferred_element_type=jnp.float32)
    c, s = tables(cosine, sine)
    for begin in range(0, product.shape[1], HD):
        turned = turn(product[:, begin : begin + HD], c, s)
        first = begin // HD * rows
        q[first : first + rows, :] = (turned * HD ** (-0.5)).astype(jnp.bfloat16)
    row_pos = rank * rows + lax.broadcasted_iota(jnp.int32, (rows, BLOCK), 0)
    first_row = jnp.zeros((rows, BLOCK), jnp.int32)
    begin = jnp.int32(0)
    for w in range(lengths.shape[0]):
        end = begin + lengths[w]
        within = (row_pos >= begin) & (row_pos < end)
        first_row = jnp.where(within, begin, first_row)
        begin = end
    is_caption = jnp.broadcast_to(caption[...], (rows, rows)).T == 1
    for order, offset in enumerate(offsets):
        block = block_of(offset)
        key_pos = block * BLOCK + lax.broadcasted_iota(jnp.int32, (rows, BLOCK), 1)
        near = (first_row <= key_pos) & (key_pos <= row_pos)
        reached = (spans[0, 0] <= block) & (block <= spans[0, 1])
        allowed = near | (is_caption & reached)
        bias[:, order * BLOCK : (order + 1) * BLOCK] = jnp.where(allowed, 0.0, -jnp.inf)
    fold(q, bias, [0], [own], scores, rounded, None, keep(state))


def middle_kernel(columns, q, bias, *refs):
    old, kv = refs[:3], refs[3 : 3 + len(columns)]
    state, (scores, rounded) = refs[3 + len(columns) : 6 + len(columns)], refs[6 + len(columns) :]
    fold(q, bias, columns, kv, scores, rounded, old, keep(state))


def last_kernel(columns, q, bias, *refs):
    old, kv = refs[:3], refs[3 : 3 + len(columns)]
    out, scores, rounded = refs[3 + len(columns) :]

    def new(head, _, highest, total, mixed):
        denominator = jnp.sum(total, -1, keepdims=True)
        out[:, head * HD : (head + 1) * HD] = (mixed / denominator).astype(jnp.bfloat16)

    fold(q, bias, columns, kv, scores, rounded, old, new)


def everywhere(
    tokens,
    norm_gain,
    query_weight,
    key_weight,
    value_weight,
    window_lengths,
    is_caption,
    span_blocks,
):
    ranks, groups = lax.axis_size("seq"), lax.axis_size("head")
    rank = lax.axis_index("seq")
    rows = tokens.shape[0]
    head_dev = query_weight.shape[1] // HD

    def move(array, shift):
        pairs = [
            (r * groups + g, (r ^ shift(g)[0]) * groups + (g ^ shift(g)[1]))
            for r in range(ranks)
            for g in range(groups)
        ]
        return lax.ppermute(array, ("seq", "head"), pairs)

    across = move(tokens, lambda g: (0, 2))
    beside = move(tokens, lambda g: (0, 1))
    features = query_weight.shape[0]
    token_copy, gain, kv_weight, wide, captions = pl.pallas_call(
        functools.partial(load_kernel, H // KV // head_dev),
        out_shape=(
            pltpu.VMEM(tokens.shape, tokens.dtype),
            pltpu.VMEM((1, features), norm_gain.dtype),
            pltpu.VMEM((features, 2 * HD), key_weight.dtype),
            pltpu.VMEM(query_weight.shape, query_weight.dtype),
            pltpu.VMEM((1, rows), is_caption.dtype),
        ),
        in_specs=[pl.BlockSpec(memory_space=pltpu.HBM)] * 6,
        out_specs=tuple(vmem(5)),
        scratch_shapes=[pltpu.SemaphoreType.DMA((6,))],
        compiler_params=grant(2),
        name="load",
    )(
        *[
            pltpu.with_memory_space_constraint(array, pltpu.HBM)
            for array in (
                tokens,
                norm_gain[None, :],
                key_weight,
                value_weight,
                query_weight,
                is_caption[None, :],
            )
        ]
    )
    half = HD // 2
    frequency = rope_base ** (-jnp.arange(half, dtype=jnp.float32) * 2.0 / HD)
    row_pos = rank * rows + jnp.arange(rows, dtype=jnp.int32)
    angles = row_pos.astype(jnp.float32)[:, None] * frequency[None, :]
    cosine, sine = near_core(jnp.cos(angles)), near_core(jnp.sin(angles))
    fourth = move(across, lambda g: (0, 1))

    squares = pl.pallas_call(
        squares_kernel,
        out_shape=pltpu.VMEM((rows, HD), jnp.float32),
        in_specs=vmem(3),
        out_specs=vmem(1)[0],
        compiler_params=grant(2),
        name="squares",
    )(near_core(token_copy), near_core(beside), near_core(across))
    key_values, normed = pl.pallas_call(
        kv_kernel,
        out_shape=(
            pltpu.VMEM((rows, 2 * HD), jnp.bfloat16),
            pltpu.VMEM((rows, features), jnp.bfloat16),
        ),
        in_specs=vmem(9),
        out_specs=tuple(vmem(2)),
        compiler_params=grant(6),
        name="keys_values",
    )(
        near_core(squares),
        near_core(token_copy),
        near_core(beside),
        near_core(across),
        near_core(fourth),
        near_core(gain),
        near_core(kv_weight),
        cosine,
        sine,
    )

    far = ranks // 2
    tall = rows * head_dev

    def swapped(array):
        return move(array, lambda g: (0, 1))

    def split(array, both):
        return move(array, lambda g: (both[g % 2], 0))

    column = split(key_values, (far, far | 2))
    row = split(key_values, (1, 2))
    corner = split(key_values, (3, 3))
    diagonal = split(key_values, (far | 1, far | 3))
    held = [
        ((0, 0), key_values),
        ((1, 2), row),
        ((far, far | 2), column),
        ((2, 1), swapped(row)),
        ((far | 2, far), swapped(column)),
        ((far | 1, far | 3), diagonal),
        ((3, 3), corner),
        ((far | 3, far | 1), swapped(diagonal)),
    ]
    offsets, arrays = [offset for offset, _ in held], [near_core(array) for _, array in held]
    state = [pltpu.VMEM((tall, BLOCK), jnp.float32)] * 2 + [pltpu.VMEM((tall, HD), jnp.float32)]

    def work(count):
        return [
            pltpu.VMEM((tall, count * BLOCK), jnp.float32),
            pltpu.VMEM((tall, count * BLOCK), jnp.bfloat16),
        ]

    q, bias, *partial = pl.pallas_call(
        functools.partial(query_kernel, offsets),
        out_shape=(
            pltpu.VMEM((tall, HD), jnp.bfloat16),
            pltpu.VMEM((rows, ranks * BLOCK), jnp.float32),
            *state,
        ),
        in_specs=smem(2) + vmem(6),
        out_specs=tuple(vmem(5)),
        scratch_shapes=work(1),
        compiler_params=grant(6),
        name="queries",
    )(
        window_lengths,
        span_blocks,
        near_core(normed),
        near_core(wide),
        cosine,
        sine,
        near_core(captions),
        arrays[0],
    )

    def columns(first, end):
        return [order * BLOCK for order in range(first, end)]

    early, later = 3, ranks - 2
    for first, end in ((1, early), (early, later)):
        partial = pl.pallas_call(
            functools.partial(middle_kernel, columns(first, end)),
            out_shape=tuple(state),
            in_specs=vmem(5 + end - first),
            out_specs=tuple(vmem(3)),
            scratch_shapes=work(end - first),
            compiler_params=grant(6),
        )(*[near_core(array) for array in (q, bias, *partial)], *arrays[first:end])
    return pl.pallas_call(
        functools.partial(last_kernel, columns(later, ranks)),
        out_shape=jax.ShapeDtypeStruct((rows, head_dev * HD), jnp.bfloat16),
        in_specs=vmem(5 + ranks - later),
        out_specs=vmem(1)[0],
        scratch_shapes=work(ranks - later),
        compiler_params=grant(6),
        name="last",
    )(*[near_core(array) for array in (q, bias, *partial)], *arrays[later:])


near_plan = (0, 1, 2, 3)
feature_plan = (0, 1, 2, 3)


def gathers_all(mesh, rows, head_dev):
    ranks, groups = mesh.shape["seq"], mesh.shape["head"]
    total_blocks = ranks * rows // BLOCK
    window = min(window_cap, total_blocks * BLOCK // 4)
    read = (window + BLOCK - 2) // BLOCK + 1 + min(span_cap, total_blocks // 4)
    shared = groups % 2 == 0 and (H // KV) % (2 * head_dev) == 0
    fits = rows == BLOCK and ranks == 2 * len(near_plan) and groups == len(feature_plan)
    return shared and fits and 2 * read >= total_blocks


def solution(mesh):
    in_specs = (P("seq", "head"), P(), P(None, "head"), P(), P(), P(), P("seq"), P("seq", None))
    out_specs = P("seq", "head")

    def per_device(*arguments):
        rows, head_dev = arguments[0].shape[0], arguments[2].shape[1] // HD
        if not gathers_all(mesh, rows, head_dev):
            return by_request(*arguments)
        return everywhere(*arguments)

    return jax.shard_map(
        per_device, mesh=mesh, in_specs=in_specs, out_specs=out_specs, check_vma=False
    )
```
